32 devices in a mesh: grp: 2 (over x), row: 16 (over z, y, core).
Axes of the slice: x: 2, y: 2, z: 4, core: 2. Of those that a mesh axis runs over, the one named last changes fastest.
Arguments:
- patches: bfloat16 [256, 32, 512], P(('grp', 'row')), parts along dimension 0, may hold values from -6 to 6
- registers: float32 [512, 512], P(('grp', 'row')), parts along dimension 0, may hold values from -6 to 6
- gain_one: float32 [512], replicated, may hold values from 0.1 to 1.9
- gain_two: float32 [512], replicated, may hold values from 0.1 to 1.9
- w_qkv_one: bfloat16 [512, 1536], replicated, may hold values from -4 to 4, as said below
- w_out_one: bfloat16 [512, 512], replicated, may hold values from -0.25 to 0.25
- w_qkv_two: bfloat16 [512, 1536], replicated, may hold values from -4 to 4, as said below
- w_out_two: bfloat16 [512, 512], replicated, may hold values from -0.25 to 0.25
Outputs:
- patches_out: bfloat16 [256, 32, 512], P(('grp', 'row')), parts along dimension 0
- registers_out: float32 [512, 512], P(('grp', 'row')), parts along dimension 0
The draws below stay inside these ranges and needn't reach their ends.
There are 2 independent parts, one for each index of `grp`. The reference program is written for one: setup_inputs(seed, part) draws one part's arguments, and reference() takes and returns one part's arrays. A program takes and returns all parts, laid end to end along the dimension named above; an argument that names none is the same for every part. Nothing has to cross between parts.
Inputs may be any that keep to these rules, and one draw needn't show every extreme that they name: `w_qkv_one`: projection weights of the query, key and value columns. `w_qkv_two`: projection weights of the query, key and value columns.
All inputs are finite; a program needn't handle non-finite values.
Results may differ from the reference program's by a relative error of at most 0.01.
Values may be sent and summed in bfloat16 or wider, within the bound.
No kernel may reach another device: no remote copies, remote signals or barrier semaphores. Data moves between devices by JAX's collectives and lax.ppermute only.
A program may use at most 128 MiB of HBM per device.

```python
import math
import jax
import jax.numpy as jnp
from jax import lax

D = 512
HEADS = 16
WIN = 8
REG = 16
H = 128
W = 32
REGS = 256
N_ROW = 16


def qkv_law(key):
    first, second, third = jax.random.split(key, 3)
    w_query = jax.random.normal(first, (D, D), jnp.float32) / math.sqrt(D)
    w_key = jax.random.normal(second, (D, D), jnp.float32) / math.sqrt(D)
    w_value = jax.random.normal(third, (D, D), jnp.float32) / math.sqrt(D)
    joined = jnp.concatenate([w_query, w_key, w_value], axis=1)
    return jnp.clip(joined, -4.0, 4.0).astype(jnp.bfloat16)


def draw_w_qkv_one(key, part):
    return qkv_law(jax.random.fold_in(key, 11))


def draw_w_qkv_two(key, part):
    return qkv_law(jax.random.fold_in(key, 12))


def levels(rng, extent, pieces, smallest, largest):
    def one(position, blocks):
        heights = jax.random.uniform(jax.random.fold_in(jax.random.fold_in(rng, 6), position), (blocks,), jnp.float32, smallest / len(pieces), largest / len(pieces))
        return jnp.repeat(jnp.exp(heights), extent[position] // blocks).reshape((-1,) + (1,) * (len(extent) - position - 1))

    factor_of = one(*pieces[0])
    for cut in pieces[1:]:
        factor_of = factor_of * one(*cut)
    return factor_of


def noise(rng, extent, scale, reach, shards=(), kind=jnp.bfloat16):
    values = scale * jax.random.normal(rng, extent, jnp.float32)
    if shards:
        values = values * levels(rng, extent, shards, -0.22, 0.18)
    return jnp.clip(values, -reach, reach).astype(kind)


def setup_inputs(seed: int = 0, part: int = 0) -> dict:
    splits = jax.random.split(jax.random.key(seed), 9)
    part_splits = jax.random.split(jax.random.fold_in(splits[8], part), 9)
    return {
        "patches": noise(part_splits[0], (H, W, D), 1.0, 6.0, ((0, 16),)),
        "registers": noise(part_splits[1], (REGS, D), 1.0, 6.0, ((0, 16),), jnp.float32),
        "gain_one": jnp.clip(1.0 + 0.18 * jax.random.normal(splits[2], (D,), jnp.float32), 0.1, 1.9),
        "gain_two": jnp.clip(1.0 + 0.18 * jax.random.normal(splits[3], (D,), jnp.float32), 0.1, 1.9),
        "w_qkv_one": draw_w_qkv_one(jax.random.fold_in(splits[8], 71), part),
        "w_out_one": noise(splits[5], (D, D), D ** -0.5, 0.25),
        "w_qkv_two": draw_w_qkv_two(jax.random.fold_in(splits[8], 71), part),
        "w_out_two": noise(splits[7], (D, D), D ** -0.5, 0.25),
    }


def layer_norm(values, gain):
    values = values.astype(jnp.float32)
    mean = lax.optimization_barrier(jnp.mean(values, -1, keepdims=True))
    centred = values - mean
    spread = lax.optimization_barrier(jnp.mean(centred * centred, -1, keepdims=True))
    return centred * lax.rsqrt(spread + 1e-05) * gain

def attend(query, keys, values):
    count, qlen, width = query.shape
    hdim = width // HEADS
    q_heads = query.reshape(count, qlen, HEADS, hdim).astype(jnp.float32)
    k_heads = keys.reshape(count, keys.shape[1], HEADS, hdim).astype(jnp.float32)
    v_heads = values.reshape(count, keys.shape[1], HEADS, hdim).astype(jnp.float32)
    scores = jnp.einsum('nqhe,nkhe->nhqk', q_heads, k_heads) / math.sqrt(hdim)
    top = lax.optimization_barrier(jnp.max(scores, -1, keepdims=True))
    expo = jnp.exp(scores - top)
    weights = (expo / lax.optimization_barrier(jnp.sum(expo, -1, keepdims=True))).astype(jnp.bfloat16)
    result = jnp.einsum('nhqk,nkhe->nqhe', weights.astype(jnp.float32), v_heads)
    return result.reshape(count, qlen, width).astype(jnp.bfloat16)

def first_band(band, reg, gain_one, gain_two, w_qkv_one, w_out_one, w_qkv_two):
    dim = D
    rows, width = (band.shape[0], band.shape[1])
    normed = layer_norm(band, gain_one).astype(jnp.bfloat16)
    qkv = jnp.dot(normed.reshape(-1, dim), w_qkv_one, preferred_element_type=jnp.float32).astype(jnp.bfloat16)
    qkv = qkv.reshape(rows, width, 3 * dim)
    reg_normed = layer_norm(reg, gain_one).astype(jnp.bfloat16)
    reg_qkv = jnp.dot(reg_normed, w_qkv_one, preferred_element_type=jnp.float32).astype(jnp.bfloat16)
    count = width // WIN
    tiles = qkv.reshape(rows, count, WIN, 3 * dim).transpose(1, 0, 2, 3).reshape(count, rows * WIN, 3 * dim)
    reg_side = jnp.broadcast_to(reg_qkv[None, :, dim:], (count, REG, 2 * dim))
    keys_all = jnp.concatenate([tiles[:, :, dim:], reg_side], 1)
    block = attend(tiles[:, :, :dim], keys_all[:, :, :dim], keys_all[:, :, dim:])
    block = block.reshape(count, rows, WIN, dim).transpose(1, 0, 2, 3).reshape(rows * width, dim)
    block_out = (band.reshape(-1, dim).astype(jnp.float32) + jnp.dot(block, w_out_one, preferred_element_type=jnp.float32)).astype(jnp.bfloat16)
    band_keys = jnp.concatenate([qkv.reshape(1, rows * width, 3 * dim)[:, :, dim:], reg_qkv[None, :, dim:]], 1)
    reg_att = attend(reg_qkv[None, :, :dim], band_keys[:, :, :dim], band_keys[:, :, dim:])[0]
    reg_out = reg + jnp.dot(reg_att, w_out_one, preferred_element_type=jnp.float32)
    reg_normed_two = layer_norm(reg_out, gain_two).astype(jnp.bfloat16)
    reg_kv = jnp.dot(reg_normed_two, w_qkv_two[:, dim:], preferred_element_type=jnp.float32).astype(jnp.bfloat16)
    normed_two = layer_norm(block_out, gain_two).astype(jnp.bfloat16)
    qkv_two = jnp.dot(normed_two, w_qkv_two, preferred_element_type=jnp.float32).astype(jnp.bfloat16)
    return (block_out.reshape(rows, width, dim), reg_out, reg_kv, qkv_two.reshape(rows, width, 3 * dim))

def reference(patches, registers, gain_one, gain_two, w_qkv_one, w_out_one, w_qkv_two, w_out_two):
    dim = D
    nrow = N_ROW
    per_band = nrow // 8
    width = W
    cls = width // WIN
    bands = patches.reshape(nrow, WIN, width, dim)
    band_regs = registers.reshape(nrow, REG, dim)

    def one_band(pair):
        return first_band(pair[0], pair[1], gain_one, gain_two, w_qkv_one, w_out_one, w_qkv_two)
    block_out, reg_out, reg_kv, qkv_two = lax.map(one_band, (bands, band_regs))
    grid_q = qkv_two.reshape(WIN, nrow, WIN, cls, 3 * dim)
    grid_y = block_out.reshape(WIN, nrow, WIN, cls, dim)
    reg_groups = reg_kv.reshape(WIN, per_band, REG, 2 * dim)

    def one_class(index):
        piece = lax.dynamic_index_in_dim(grid_q, index, 1, keepdims=False)
        piece = piece.transpose(2, 0, 1, 3).reshape(cls, WIN * WIN, 3 * dim)
        resid = lax.dynamic_index_in_dim(grid_y, index, 1, keepdims=False)
        resid = resid.transpose(2, 0, 1, 3).reshape(cls, WIN * WIN, dim)
        regs = lax.dynamic_index_in_dim(reg_groups, index // 8, 1, keepdims=False).reshape(WIN * REG, 2 * dim)
        regs = jnp.broadcast_to(regs[None], (cls, WIN * REG, 2 * dim))
        keys = jnp.concatenate([piece[:, :, dim:2 * dim], regs[:, :, :dim]], 1)
        vals = jnp.concatenate([piece[:, :, 2 * dim:], regs[:, :, dim:]], 1)
        att = attend(piece[:, :, :dim], keys, vals)
        result = (resid.reshape(-1, dim).astype(jnp.float32) + jnp.dot(att.reshape(-1, dim), w_out_two, preferred_element_type=jnp.float32)).astype(jnp.bfloat16)
        return result.reshape(cls, WIN, WIN, dim).transpose(1, 2, 0, 3)
    outs = lax.map(one_class, jnp.arange(nrow, dtype=jnp.int32))
    patches_out = outs.transpose(1, 0, 2, 3, 4).reshape(WIN * nrow, width, dim)
    return (patches_out, reg_out.reshape(nrow * REG, dim))
```

```python
import functools
import math

import jax
import jax.numpy as jnp
from jax import lax
from jax.experimental import pallas as pl
from jax.experimental.pallas import tpu as pltpu
from jax.sharding import PartitionSpec as P

HEADS = 16
WIN = 8
REG = 16
LANES = 128

NT = (((1,), (1,)), ((), ()))
TN = (((0,), (0,)), ((), ()))
NN = (((1,), (0,)), ((), ()))


def dot(lhs, rhs, dims=NN):
    return lax.dot_general(lhs, rhs, dims, preferred_element_type=jnp.float32)


def layer_norm(values, gain):
    mean = jnp.mean(values, -1, keepdims=True)
    centred = values - mean
    spread = jnp.mean(centred * centred, -1, keepdims=True)
    return centred * lax.rsqrt(spread + 1e-05) * gain


def head_mask(qlen, hdim):
    per = LANES // hdim
    row = lax.broadcasted_iota(jnp.int32, (per * qlen, LANES), 0) // qlen
    lane = lax.broadcasted_iota(jnp.int32, (per * qlen, LANES), 1) // hdim
    return jnp.where(row == lane, 1.0, 0.0).astype(jnp.bfloat16)


def attend_group(query, keys, values, mask, hdim):
    per = LANES // hdim
    stacked = jnp.concatenate([query] * per, 0) * mask
    scores = dot(keys, stacked, NT)
    top = jnp.max(scores, 0, keepdims=True)
    expo = jnp.exp2((scores - top) * (math.log2(math.e) / math.sqrt(hdim)))
    total = jnp.sum(expo, 0, keepdims=True)
    mixed = dot(values, expo.astype(jnp.bfloat16), TN)
    return mixed * (1.0 / total)


def pick_heads(mixed, qlen, hdim):
    per = LANES // hdim
    return jnp.concatenate(
        [mixed[h * hdim : (h + 1) * hdim, h * qlen : (h + 1) * qlen] for h in range(per)], 0
    )


def block_kernel(x_ref, reg_ref, gain_ref, wqkv_ref, wout_ref, out_ref, kv_ref, rqkv_ref):
    rows, width, dim = x_ref.shape
    hdim = dim // HEADS
    count = width // WIN
    gain = gain_ref[...]
    values = x_ref[...].astype(jnp.float32)
    tokens = jnp.concatenate(
        [values[:, w * WIN : (w + 1) * WIN, :].reshape(rows * WIN, dim) for w in range(count)], 0
    )
    normed = layer_norm(tokens, gain).astype(jnp.bfloat16)
    reg_normed = layer_norm(reg_ref[...], gain).astype(jnp.bfloat16)
    qkv = dot(normed, wqkv_ref[...]).astype(jnp.bfloat16)
    reg_qkv = dot(reg_normed, wqkv_ref[...]).astype(jnp.bfloat16)
    kv_ref[...] = qkv[:, dim:]
    rqkv_ref[...] = reg_qkv
    qlen = rows * WIN
    mask = head_mask(qlen, hdim)
    atts = []
    for w in range(count):
        own = qkv[w * qlen : (w + 1) * qlen]
        parts = []
        for g in range(dim // LANES):
            q0, k0, v0 = (g * LANES + j * dim for j in range(3))
            keys = jnp.concatenate([own[:, k0 : k0 + LANES], reg_qkv[:, k0 : k0 + LANES]], 0)
            vals = jnp.concatenate([own[:, v0 : v0 + LANES], reg_qkv[:, v0 : v0 + LANES]], 0)
            mixed = attend_group(own[:, q0 : q0 + LANES], keys, vals, mask, hdim)
            parts.append(pick_heads(mixed, qlen, hdim))
        atts.append(jnp.concatenate(parts, 0).T.astype(jnp.bfloat16))
    att = jnp.concatenate(atts, 0)
    result = tokens + dot(att, wout_ref[...])
    for w in range(count):
        piece = result[w * qlen : (w + 1) * qlen].reshape(rows, WIN, dim)
        out_ref[:, w * WIN : (w + 1) * WIN, :] = piece.astype(jnp.bfloat16)


def register_kernel(kv_ref, rqkv_ref, reg_ref, gain_ref, wout_ref, out_ref, normed_ref):
    dim = reg_ref.shape[1]
    hdim = dim // HEADS
    rqkv = rqkv_ref[...]
    kv = kv_ref[...]
    mask = head_mask(REG, hdim)
    parts = []
    for g in range(dim // LANES):
        lo = g * LANES
        keys = jnp.concatenate([kv[:, lo : lo + LANES], rqkv[:, dim + lo : dim + lo + LANES]], 0)
        vals = jnp.concatenate(
            [kv[:, dim + lo : dim + lo + LANES], rqkv[:, 2 * dim + lo : 2 * dim + lo + LANES]], 0
        )
        mixed = attend_group(rqkv[:, lo : lo + LANES], keys, vals, mask, hdim)
        parts.append(pick_heads(mixed, REG, hdim))
    att = jnp.concatenate(parts, 0).T.astype(jnp.bfloat16)
    result = reg_ref[...] + dot(att, wout_ref[...])
    out_ref[...] = result
    normed_ref[...] = layer_norm(result, gain_ref[...]).astype(jnp.bfloat16)


def grid_kernel(x_ref, r0, r1, r2, r3, gain_ref, wqkv_ref, wout_ref, out_ref, scratch):
    total, dim = x_ref.shape
    width = total // WIN
    cls = width // WIN
    hdim = dim // HEADS
    qlen = WIN * WIN
    step = 4 if cls % 4 == 0 else 1
    gain = gain_ref[...]
    regs = jnp.concatenate([r0[...], r1[...], r2[...], r3[...]], 0)
    reg_kv = dot(regs, wqkv_ref[:, dim:]).astype(jnp.bfloat16)
    mask = head_mask(qlen, hdim)
    lanes = [slice(g * LANES, (g + 1) * LANES) for g in range(dim // LANES)]
    for g, part in enumerate(lanes):
        scratch[g] = x_ref[:, part].astype(jnp.float32)
    for first in range(0, cls, step):
        starts = [a * width + first + c for c in range(step) for a in range(WIN)]
        tokens = jnp.concatenate(
            [
                jnp.concatenate(
                    [scratch[g, pl.ds(start, WIN, stride=cls), :] for start in starts], 0
                )
                for g in range(len(lanes))
            ],
            1,
        )
        normed = layer_norm(tokens, gain).astype(jnp.bfloat16)
        qkv = dot(normed, wqkv_ref[...]).astype(jnp.bfloat16)
        atts = []
        for c in range(step):
            own = qkv[c * qlen : (c + 1) * qlen]
            parts = []
            for g in range(dim // LANES):
                q0, k0, v0 = (g * LANES + j * dim for j in range(3))
                keys = jnp.concatenate(
                    [own[:, k0 : k0 + LANES], reg_kv[:, k0 - dim : k0 - dim + LANES]], 0
                )
                vals = jnp.concatenate(
                    [own[:, v0 : v0 + LANES], reg_kv[:, v0 - dim : v0 - dim + LANES]], 0
                )
                mixed = attend_group(own[:, q0 : q0 + LANES], keys, vals, mask, hdim)
                parts.append(pick_heads(mixed, qlen, hdim))
            atts.append(jnp.concatenate(parts, 0).T.astype(jnp.bfloat16))
        result = tokens + dot(jnp.concatenate(atts, 0), wout_ref[...])
        for i, start in enumerate(starts):
            for g, part in enumerate(lanes):
                scratch[g, pl.ds(start, WIN, stride=cls), :] = result[i * WIN : (i + 1) * WIN, part]
    for g, part in enumerate(lanes):
        out_ref[:, part] = scratch[g].astype(jnp.bfloat16)


def call(kernel, outs, scratch=(), flops=0):
    return pl.pallas_call(
        kernel,
        out_shape=outs,
        scratch_shapes=list(scratch),
        compiler_params=pltpu.CompilerParams(vmem_limit_bytes=40 << 20),
        cost_estimate=pl.CostEstimate(flops=flops, bytes_accessed=4 << 20, transcendentals=0),
    )


def on_device(patches, registers, gain_one, gain_two, w_qkv_one, w_out_one, w_qkv_two, w_out_two):
    rows, width, dim = patches.shape
    nrow = lax.axis_size("row")
    per_band = nrow // WIN
    count = rows * width
    groups = [[a * per_band + p for a in range(WIN)] for p in range(per_band)]

    def swap(values, bit):
        pairs = [
            (a * per_band + p, (a ^ bit) * per_band + p) for a in range(WIN) for p in range(per_band)
        ]
        return lax.ppermute(values, "row", pairs)

    def exchange(values):
        return lax.all_to_all(
            values, "row", 0, 0, axis_index_groups=groups, tiled=True
        )

    bf16, f32 = jnp.bfloat16, jnp.float32
    shape = jax.ShapeDtypeStruct
    g_one, g_two = gain_one.reshape(1, dim), gain_two.reshape(1, dim)
    block_out, kv, rqkv = call(
        block_kernel,
        (
            shape((rows, width, dim), bf16),
            shape((count, 2 * dim), bf16),
            shape((REG, 3 * dim), bf16),
        ),
        flops=2 * count * dim * 4 * dim,
    )(patches, registers, g_one, w_qkv_one, w_out_one)
    reg_out, r0 = call(
        register_kernel, (shape((REG, dim), f32), shape((REG, dim), bf16)), flops=200_000_000
    )(kv, rqkv, registers, g_two, w_out_one)
    r1 = swap(r0, 1)
    r2 = swap(jnp.concatenate([r0, r1], 0), 2)
    r3 = swap(jnp.concatenate([r0, r1, r2], 0), 4)
    arrived = exchange(block_out)
    finished = call(
        grid_kernel,
        shape((count, dim), bf16),
        [pltpu.VMEM((dim // LANES, count, LANES), f32)],
        flops=2 * count * dim * 6 * dim,
    )(arrived.reshape(count, dim), r0, r1, r2, r3, g_two, w_qkv_two, w_out_two)
    patches_out = exchange(finished.reshape(rows, width, dim))
    return (patches_out, reg_out)


def solution(mesh):
    in_specs = (
        P(("grp", "row"), None, None),
        P(("grp", "row"), None),
        P(),
        P(),
        P(),
        P(),
        P(),
        P(),
    )
    out_specs = (P(("grp", "row"), None, None), P(("grp", "row"), None))
    return jax.shard_map(
        on_device, mesh=mesh, in_specs=in_specs, out_specs=out_specs, check_vma=False
    )
```

```python
import functools
import math

import jax
import jax.numpy as jnp
from jax import lax
from jax.experimental import pallas as pl
from jax.experimental.pallas import tpu as pltpu
from jax.sharding import PartitionSpec as P

HEADS = 16
WIN = 8
REG = 16
LANES = 128

NT = (((1,), (1,)), ((), ()))
TN = (((0,), (0,)), ((), ()))
NN = (((1,), (0,)), ((), ()))


def dot(lhs, rhs, dims=NN):
    return lax.dot_general(lhs, rhs, dims, preferred_element_type=jnp.float32)


def layer_norm(values, gain):
    mean = jnp.mean(values, -1, keepdims=True)
    centred = values - mean
    spread = jnp.mean(centred * centred, -1, keepdims=True)
    return centred * lax.rsqrt(spread + 1e-05) * gain


def head_mask(qlen, hdim):
    per = LANES // hdim
    row = lax.broadcasted_iota(jnp.int32, (per * qlen, LANES), 0) // qlen
    lane = lax.broadcasted_iota(jnp.int32, (per * qlen, LANES), 1) // hdim
    return jnp.where(row == lane, 1.0, 0.0).astype(jnp.bfloat16)


def attend_group(query, keys, values, mask, hdim):
    per = LANES // hdim
    stacked = jnp.concatenate([query] * per, 0) * mask
    scores = dot(keys, stacked, NT)
    top = jnp.max(scores, 0, keepdims=True)
    expo = jnp.exp2((scores - top) * (math.log2(math.e) / math.sqrt(hdim)))
    total = jnp.sum(expo, 0, keepdims=True)
    mixed = dot(values, expo.astype(jnp.bfloat16), TN)
    return mixed * (1.0 / total)


def pick_heads(mixed, qlen, hdim):
    per = LANES // hdim
    return jnp.concatenate(
        [mixed[h * hdim : (h + 1) * hdim, h * qlen : (h + 1) * qlen] for h in range(per)], 0
    )


def register_attention(query, keys, values, hdim):
    dim = query.shape[1]
    mask = head_mask(REG, hdim)
    per = LANES // hdim
    scores = []
    for lo in range(0, dim, LANES):
        stacked = jnp.concatenate([query[:, lo : lo + LANES]] * per, 0) * mask
        scores.append(dot(keys[:, lo : lo + LANES], stacked, NT))
    scores = jnp.concatenate(scores, 1)
    top = jnp.max(scores, 0, keepdims=True)
    expo = jnp.exp2((scores - top) * (math.log2(math.e) / math.sqrt(hdim)))
    weights = (expo * (1.0 / jnp.sum(expo, 0, keepdims=True))).astype(jnp.bfloat16)
    mixed = dot(weights, values, TN)
    lane = lax.broadcasted_iota(jnp.int32, (REG, dim), 1) // hdim
    result = jnp.zeros((REG, dim), jnp.float32)
    for h in range(HEADS):
        result = jnp.where(lane == h, mixed[h * REG : (h + 1) * REG], result)
    return result.astype(jnp.bfloat16)


def block_kernel(
    x_hbm, reg_hbm, gain_hbm, gain_two_hbm, wqkv_hbm, wout_hbm,
    out_ref, reg_out_ref,
    x_ref, reg_ref, gain_ref, gain_two_ref, wqkv_ref, wout_ref, sems,
):
    pairs = [
        (x_hbm, x_ref), (reg_hbm, reg_ref), (gain_hbm, gain_ref),
        (wqkv_hbm, wqkv_ref), (wout_hbm, wout_ref), (gain_two_hbm, gain_two_ref),
    ]
    copies = [pltpu.make_async_copy(src, dst, sems.at[i]) for i, (src, dst) in enumerate(pairs)]
    for copy in copies:
        copy.start()
    for copy in copies[:3]:
        copy.wait()
    rows, width, dim = x_ref.shape
    hdim = dim // HEADS
    count = width // WIN
    gain = gain_ref[...]
    values = x_ref[...].astype(jnp.float32)
    tokens = jnp.concatenate(
        [values[:, w * WIN : (w + 1) * WIN, :].reshape(rows * WIN, dim) for w in range(count)], 0
    )
    normed = layer_norm(tokens, gain).astype(jnp.bfloat16)
    reg_normed = layer_norm(reg_ref[...], gain).astype(jnp.bfloat16)
    copies[3].wait()
    qkv = dot(normed, wqkv_ref[...]).astype(jnp.bfloat16)
    reg_qkv = dot(reg_normed, wqkv_ref[...]).astype(jnp.bfloat16)
    reg_att = register_attention(
        reg_qkv[:, :dim],
        jnp.concatenate([qkv[:, dim : 2 * dim], reg_qkv[:, dim : 2 * dim]], 0),
        jnp.concatenate([qkv[:, 2 * dim :], reg_qkv[:, 2 * dim :]], 0),
        hdim,
    )
    copies[4].wait()
    copies[5].wait()
    reg_out = reg_ref[...] + dot(reg_att, wout_ref[...])
    reg_out_ref[...] = reg_out
    travelling = layer_norm(reg_out, gain_two_ref[...]).astype(jnp.bfloat16)
    for r in range(rows):
        out_ref[r, width:, :] = travelling
    qlen = rows * WIN
    mask = head_mask(qlen, hdim)
    atts = []
    for w in range(count):
        own = qkv[w * qlen : (w + 1) * qlen]
        parts = []
        for g in range(dim // LANES):
            q0, k0, v0 = (g * LANES + j * dim for j in range(3))
            keys = jnp.concatenate([own[:, k0 : k0 + LANES], reg_qkv[:, k0 : k0 + LANES]], 0)
            vals = jnp.concatenate([own[:, v0 : v0 + LANES], reg_qkv[:, v0 : v0 + LANES]], 0)
            mixed = attend_group(own[:, q0 : q0 + LANES], keys, vals, mask, hdim)
            parts.append(pick_heads(mixed, qlen, hdim))
        atts.append(jnp.concatenate(parts, 0).T.astype(jnp.bfloat16))
    att = jnp.concatenate(atts, 0)
    result = tokens + dot(att, wout_ref[...])
    for w in range(count):
        piece = result[w * qlen : (w + 1) * qlen].reshape(rows, WIN, dim)
        out_ref[:, w * WIN : (w + 1) * WIN, :] = piece.astype(jnp.bfloat16)


def grid_kernel(x_ref, gain_ref, wqkv_ref, wout_ref, out_ref, scratch):
    _, width, dim = out_ref.shape
    cls = width // WIN
    hdim = dim // HEADS
    qlen = WIN * WIN
    step = 4 if cls % 4 == 0 else 1
    gain = gain_ref[...]
    regs = jnp.concatenate([x_ref[a, width:, :] for a in range(WIN)], 0)
    reg_kv = dot(regs, wqkv_ref[:, dim:]).astype(jnp.bfloat16)
    mask = head_mask(qlen, hdim)
    lanes = [slice(g * LANES, (g + 1) * LANES) for g in range(dim // LANES)]
    for g, part in enumerate(lanes):
        for a in range(WIN):
            scratch[g, a * width : (a + 1) * width] = x_ref[a, :width, part].astype(jnp.float32)
    for first in range(0, cls, step):
        starts = [a * width + first + c for c in range(step) for a in range(WIN)]
        tokens = jnp.concatenate(
            [
                jnp.concatenate(
                    [scratch[g, pl.ds(start, WIN, stride=cls), :] for start in starts], 0
                )
                for g in range(len(lanes))
            ],
            1,
        )
        normed = layer_norm(tokens, gain).astype(jnp.bfloat16)
        qkv = dot(normed, wqkv_ref[...]).astype(jnp.bfloat16)
        atts = []
        for c in range(step):
            own = qkv[c * qlen : (c + 1) * qlen]
            parts = []
            for g in range(dim // LANES):
                q0, k0, v0 = (g * LANES + j * dim for j in range(3))
                keys = jnp.concatenate(
                    [own[:, k0 : k0 + LANES], reg_kv[:, k0 - dim : k0 - dim + LANES]], 0
                )
                vals = jnp.concatenate(
                    [own[:, v0 : v0 + LANES], reg_kv[:, v0 - dim : v0 - dim + LANES]], 0
                )
                mixed = attend_group(own[:, q0 : q0 + LANES], keys, vals, mask, hdim)
                parts.append(pick_heads(mixed, qlen, hdim))
            atts.append(jnp.concatenate(parts, 0).T.astype(jnp.bfloat16))
        result = tokens + dot(jnp.concatenate(atts, 0), wout_ref[...])
        for i, start in enumerate(starts):
            for g, part in enumerate(lanes):
                scratch[g, pl.ds(start, WIN, stride=cls), :] = result[i * WIN : (i + 1) * WIN, part]
    for g, part in enumerate(lanes):
        for a in range(WIN):
            out_ref[a, :, part] = scratch[g, a * width : (a + 1) * width].astype(jnp.bfloat16)


def call(kernel, outs, scratch=(), flops=0, in_specs=None):
    specs = {} if in_specs is None else {"in_specs": in_specs}
    return pl.pallas_call(
        kernel,
        out_shape=outs,
        scratch_shapes=list(scratch),
        compiler_params=pltpu.CompilerParams(vmem_limit_bytes=40 << 20),
        cost_estimate=pl.CostEstimate(flops=flops, bytes_accessed=4 << 20, transcendentals=0),
        **specs,
    )


def on_device(patches, registers, gain_one, gain_two, w_qkv_one, w_out_one, w_qkv_two, w_out_two):
    rows, width, dim = patches.shape
    nrow = lax.axis_size("row")
    per_band = nrow // WIN
    count = rows * width
    groups = [[a * per_band + p for a in range(WIN)] for p in range(per_band)]

    def exchange(values):
        return lax.all_to_all(
            values, "row", 0, 0, axis_index_groups=groups, tiled=True
        )

    bf16, f32 = jnp.bfloat16, jnp.float32
    shape = jax.ShapeDtypeStruct
    g_one, g_two = gain_one.reshape(1, dim), gain_two.reshape(1, dim)
    fetched = [
        pltpu.with_memory_space_constraint(value, pltpu.MemorySpace.HBM)
        for value in (patches, registers, g_one, g_two, w_qkv_one, w_out_one)
    ]
    outgoing, reg_out = call(
        block_kernel,
        (shape((rows, width + REG, dim), bf16), shape((REG, dim), f32)),
        [
            pltpu.VMEM((rows, width, dim), bf16),
            pltpu.VMEM((REG, dim), f32),
            pltpu.VMEM((1, dim), f32),
            pltpu.VMEM((1, dim), f32),
            pltpu.VMEM((dim, 3 * dim), bf16),
            pltpu.VMEM((dim, dim), bf16),
            pltpu.SemaphoreType.DMA((6,)),
        ],
        flops=2 * count * dim * 4 * dim,
        in_specs=[pl.BlockSpec(memory_space=pltpu.MemorySpace.HBM)] * 6,
    )(*fetched)
    finished = call(
        grid_kernel,
        shape((rows, width, dim), bf16),
        [pltpu.VMEM((dim // LANES, count, LANES), f32)],
        flops=2 * count * dim * 6 * dim,
    )(exchange(outgoing), g_two, w_qkv_two, w_out_two)
    patches_out = exchange(finished)
    return (patches_out, reg_out)


def solution(mesh):
    in_specs = (
        P(("grp", "row"), None, None),
        P(("grp", "row"), None),
        P(),
        P(),
        P(),
        P(),
        P(),
        P(),
    )
    out_specs = (P(("grp", "row"), None, None), P(("grp", "row"), None))
    return jax.shard_map(
        on_device, mesh=mesh, in_specs=in_specs, out_specs=out_specs, check_vma=False
    )
```

```python
import functools
import math

import jax
import jax.numpy as jnp
from jax import lax
from jax.experimental import pallas as pl
from jax.experimental.pallas import tpu as pltpu
from jax.sharding import PartitionSpec as P

HEADS = 16
WIN = 8
REG = 16
LANES = 128

NT = (((1,), (1,)), ((), ()))
TN = (((0,), (0,)), ((), ()))
NN = (((1,), (0,)), ((), ()))


def dot(lhs, rhs, dims=NN):
    return lax.dot_general(lhs, rhs, dims, preferred_element_type=jnp.float32)


def layer_norm(values, gain):
    mean = jnp.mean(values, -1, keepdims=True)
    centred = values - mean
    spread = jnp.mean(centred * centred, -1, keepdims=True)
    return centred * lax.rsqrt(spread + 1e-05) * gain


def head_mask(qlen, hdim):
    per = LANES // hdim
    row = lax.broadcasted_iota(jnp.int32, (per * qlen, LANES), 0) // qlen
    lane = lax.broadcasted_iota(jnp.int32, (per * qlen, LANES), 1) // hdim
    return jnp.where(row == lane, 1.0, 0.0).astype(jnp.bfloat16)


def pick_heads(mixed, qlen, hdim):
    return jnp.concatenate(
        [
            mixed[h * hdim : (h + 1) * hdim, h * qlen : (h + 1) * qlen]
            for h in range(LANES // hdim)
        ],
        0,
    )


def attend_windows(qkv, reg_keys, reg_values, windows, qlen, mask, hdim):
    dim = reg_keys.shape[1]
    units = [(w, slice(lo, lo + LANES)) for w in windows for lo in range(0, dim, LANES)]
    tops, totals, done, held, weights = {}, {}, {}, {}, {}

    def scores(n):
        w, part = units[n]
        own = qkv[w * qlen : (w + 1) * qlen]
        keys = jnp.concatenate([own[:, dim : 2 * dim][:, part], reg_keys[:, part]], 0)
        stacked = jnp.concatenate([own[:, part]] * (LANES // hdim), 0) * mask
        result = dot(keys, stacked, NT)
        held[n] = result
        tops[n] = jnp.max(result, 0, keepdims=True)

    def exponentials(n):
        scale = math.log2(math.e) / math.sqrt(hdim)
        expo = jnp.exp2((held.pop(n) - tops[n]) * scale)
        totals[n] = 1.0 / jnp.sum(expo, 0, keepdims=True)
        weights[n] = expo.astype(jnp.bfloat16)

    def weighted(n):
        w, part = units[n]
        own = qkv[w * qlen : (w + 1) * qlen]
        values = jnp.concatenate([own[:, 2 * dim :][:, part], reg_values[:, part]], 0)
        mixed = dot(values, weights.pop(n), TN) * totals[n]
        done[n] = pick_heads(mixed, qlen, hdim)

    for n in range(len(units) + 8):
        if n < len(units):
            scores(n)
        if 0 <= n - 4 < len(units):
            exponentials(n - 4)
        if 0 <= n - 8:
            weighted(n - 8)
    per = dim // LANES
    return [
        jnp.concatenate([done[i * per + g] for g in range(per)], 0) for i in range(len(windows))
    ]


def register_attention(query, keys, values, hdim):
    dim = query.shape[1]
    mask = head_mask(REG, hdim)
    per = LANES // hdim
    scores = []
    for lo in range(0, dim, LANES):
        stacked = jnp.concatenate([query[:, lo : lo + LANES]] * per, 0) * mask
        scores.append(dot(keys[:, lo : lo + LANES], stacked, NT))
    scores = jnp.concatenate(scores, 1)
    top = jnp.max(scores, 0, keepdims=True)
    expo = jnp.exp2((scores - top) * (math.log2(math.e) / math.sqrt(hdim)))
    weights = (expo * (1.0 / jnp.sum(expo, 0, keepdims=True))).astype(jnp.bfloat16)
    mixed = dot(weights, values, TN)
    lane = lax.broadcasted_iota(jnp.int32, (REG, dim), 1) // hdim
    result = jnp.zeros((REG, dim), jnp.float32)
    for h in range(HEADS):
        result = jnp.where(lane == h, mixed[h * REG : (h + 1) * REG], result)
    return result.astype(jnp.bfloat16)


def block_kernel(
    x_hbm, reg_hbm, gain_hbm, gain_two_hbm, wqkv_hbm, wout_hbm,
    out_ref, reg_out_ref,
    x_ref, reg_ref, gain_ref, gain_two_ref, wqkv_ref, wout_ref, sems,
):
    pairs = [
        (x_hbm, x_ref), (reg_hbm, reg_ref), (gain_hbm, gain_ref),
        (wqkv_hbm, wqkv_ref), (wout_hbm, wout_ref), (gain_two_hbm, gain_two_ref),
    ]
    copies = [pltpu.make_async_copy(src, dst, sems.at[i]) for i, (src, dst) in enumerate(pairs)]
    for copy in copies:
        copy.start()
    for copy in copies[:3]:
        copy.wait()
    rows, width, dim = x_ref.shape
    hdim = dim // HEADS
    count = width // WIN
    gain = gain_ref[...]
    values = x_ref[...].astype(jnp.float32)
    tokens = jnp.concatenate(
        [values[:, w * WIN : (w + 1) * WIN, :].reshape(rows * WIN, dim) for w in range(count)], 0
    )
    normed = layer_norm(tokens, gain).astype(jnp.bfloat16)
    reg_normed = layer_norm(reg_ref[...], gain).astype(jnp.bfloat16)
    for copy in copies[3:]:
        copy.wait()
    qkv = dot(normed, wqkv_ref[...]).astype(jnp.bfloat16)
    reg_qkv = dot(reg_normed, wqkv_ref[...]).astype(jnp.bfloat16)
    reg_att = register_attention(
        reg_qkv[:, :dim],
        jnp.concatenate([qkv[:, dim : 2 * dim], reg_qkv[:, dim : 2 * dim]], 0),
        jnp.concatenate([qkv[:, 2 * dim :], reg_qkv[:, 2 * dim :]], 0),
        hdim,
    )
    reg_out = reg_ref[...] + dot(reg_att, wout_ref[...])
    reg_out_ref[...] = reg_out
    travelling = layer_norm(reg_out, gain_two_ref[...]).astype(jnp.bfloat16)
    for r in range(rows):
        out_ref[r, width:, :] = travelling
    qlen = rows * WIN
    mask = head_mask(qlen, hdim)
    reg_keys, reg_values = reg_qkv[:, dim : 2 * dim], reg_qkv[:, 2 * dim :]
    atts = attend_windows(
        qkv, reg_keys, reg_values, range(count), qlen, mask, hdim
    )
    att = jnp.concatenate([each.T.astype(jnp.bfloat16) for each in atts], 0)
    result = tokens + dot(att, wout_ref[...])
    for w in range(count):
        piece = result[w * qlen : (w + 1) * qlen].reshape(rows, WIN, dim)
        out_ref[:, w * WIN : (w + 1) * WIN, :] = piece.astype(jnp.bfloat16)


def grid_kernel(x_ref, gain_ref, wqkv_ref, wout_ref, out_ref, scratch):
    _, width, dim = out_ref.shape
    cls = width // WIN
    hdim = dim // HEADS
    qlen = WIN * WIN
    step = 4 if cls % 4 == 0 else 1
    gain = gain_ref[...]
    regs = jnp.concatenate([x_ref[a, width:, :] for a in range(WIN)], 0)
    reg_kv = dot(regs, wqkv_ref[:, dim:]).astype(jnp.bfloat16)
    mask = head_mask(qlen, hdim)
    lanes = [slice(g * LANES, (g + 1) * LANES) for g in range(dim // LANES)]
    for g, part in enumerate(lanes):
        for a in range(WIN):
            scratch[g, a * width : (a + 1) * width] = x_ref[a, :width, part].astype(jnp.float32)
    for first in range(0, cls, step):
        starts = [a * width + first + c for c in range(step) for a in range(WIN)]
        tokens = jnp.concatenate(
            [
                jnp.concatenate(
                    [scratch[g, pl.ds(start, WIN, stride=cls), :] for start in starts], 0
                )
                for g in range(len(lanes))
            ],
            1,
        )
        normed = layer_norm(tokens, gain).astype(jnp.bfloat16)
        qkv = dot(normed, wqkv_ref[...]).astype(jnp.bfloat16)
        atts = attend_windows(
            qkv, reg_kv[:, :dim], reg_kv[:, dim:], range(step), qlen, mask, hdim
        )
        att = jnp.concatenate([each.T.astype(jnp.bfloat16) for each in atts], 0)
        result = tokens + dot(att, wout_ref[...])
        for i, start in enumerate(starts):
            for g, part in enumerate(lanes):
                scratch[g, pl.ds(start, WIN, stride=cls), :] = result[i * WIN : (i + 1) * WIN, part]
    for g, part in enumerate(lanes):
        for a in range(WIN):
            out_ref[a, :, part] = scratch[g, a * width : (a + 1) * width].astype(jnp.bfloat16)


def call(kernel, outs, scratch=(), flops=0, in_specs=None):
    specs = {} if in_specs is None else {"in_specs": in_specs}
    return pl.pallas_call(
        kernel,
        out_shape=outs,
        scratch_shapes=list(scratch),
        compiler_params=pltpu.CompilerParams(vmem_limit_bytes=40 << 20),
        cost_estimate=pl.CostEstimate(flops=flops, bytes_accessed=4 << 20, transcendentals=0),
        **specs,
    )


def on_device(patches, registers, gain_one, gain_two, w_qkv_one, w_out_one, w_qkv_two, w_out_two):
    rows, width, dim = patches.shape
    nrow = lax.axis_size("row")
    per_band = nrow // WIN
    count = rows * width
    groups = [[a * per_band + p for a in range(WIN)] for p in range(per_band)]

    def exchange(values):
        return lax.all_to_all(
            values, "row", 0, 0, axis_index_groups=groups, tiled=True
        )

    bf16, f32 = jnp.bfloat16, jnp.float32
    shape = jax.ShapeDtypeStruct
    g_one, g_two = gain_one.reshape(1, dim), gain_two.reshape(1, dim)
    fetched = [
        pltpu.with_memory_space_constraint(value, pltpu.MemorySpace.HBM)
        for value in (patches, registers, g_one, g_two, w_qkv_one, w_out_one)
    ]
    outgoing, reg_out = call(
        block_kernel,
        (shape((rows, width + REG, dim), bf16), shape((REG, dim), f32)),
        [
            pltpu.VMEM((rows, width, dim), bf16),
            pltpu.VMEM((REG, dim), f32),
            pltpu.VMEM((1, dim), f32),
            pltpu.VMEM((1, dim), f32),
            pltpu.VMEM((dim, 3 * dim), bf16),
            pltpu.VMEM((dim, dim), bf16),
            pltpu.SemaphoreType.DMA((6,)),
        ],
        flops=2 * count * dim * 4 * dim,
        in_specs=[pl.BlockSpec(memory_space=pltpu.MemorySpace.HBM)] * 6,
    )(*fetched)
    finished = call(
        grid_kernel,
        shape((rows, width, dim), bf16),
        [
            pltpu.VMEM((dim // LANES, count, LANES), f32),
        ],
        flops=2 * count * dim * 6 * dim,
    )(exchange(outgoing), g_two, w_qkv_two, w_out_two)
    patches_out = exchange(finished)
    return (patches_out, reg_out)


def solution(mesh):
    in_specs = (
        P(("grp", "row"), None, None),
        P(("grp", "row"), None),
        P(),
        P(),
        P(),
        P(),
        P(),
        P(),
    )
    out_specs = (P(("grp", "row"), None, None), P(("grp", "row"), None))
    return jax.shard_map(
        on_device, mesh=mesh, in_specs=in_specs, out_specs=out_specs, check_vma=False
    )
```

```python
import functools
import math

import jax
import jax.numpy as jnp
from jax import lax
from jax.experimental import pallas as pl
from jax.experimental.pallas import tpu as pltpu
from jax.sharding import PartitionSpec as P

HEADS = 16
WIN = 8
REG = 16
LANES = 128
ORDER = (5, 4, 1, 0, 7, 6, 3, 2)

NT = (((1,), (1,)), ((), ()))
TN = (((0,), (0,)), ((), ()))
NN = (((1,), (0,)), ((), ()))


def dot(lhs, rhs, dims=NN):
    return lax.dot_general(lhs, rhs, dims, preferred_element_type=jnp.float32)


def layer_norm(values, gain):
    mean = jnp.mean(values, -1, keepdims=True)
    centred = values - mean
    spread = jnp.mean(centred * centred, -1, keepdims=True)
    return centred * lax.rsqrt(spread + 1e-05) * gain


def head_mask(qlen, hdim):
    per = LANES // hdim
    row = lax.broadcasted_iota(jnp.int32, (per * qlen, LANES), 0) // qlen
    lane = lax.broadcasted_iota(jnp.int32, (per * qlen, LANES), 1) // hdim
    return jnp.where(row == lane, 1.0, 0.0).astype(jnp.bfloat16)


def pick_heads(mixed, qlen, hdim):
    return jnp.concatenate(
        [
            mixed[h * hdim : (h + 1) * hdim, h * qlen : (h + 1) * qlen]
            for h in range(LANES // hdim)
        ],
        0,
    )


def attend_windows(qkv, reg_keys, reg_values, windows, qlen, mask, hdim):
    dim = reg_keys.shape[1]
    units = [(w, slice(lo, lo + LANES)) for w in windows for lo in range(0, dim, LANES)]
    tops, totals, done, held, weights = {}, {}, {}, {}, {}

    def scores(n):
        w, part = units[n]
        own = qkv[w * qlen : (w + 1) * qlen]
        keys = jnp.concatenate([own[:, dim : 2 * dim][:, part], reg_keys[:, part]], 0)
        stacked = jnp.concatenate([own[:, part]] * (LANES // hdim), 0) * mask
        result = dot(keys, stacked, NT)
        held[n] = result
        tops[n] = jnp.max(result, 0, keepdims=True)

    def exponentials(n):
        scale = math.log2(math.e) / math.sqrt(hdim)
        expo = jnp.exp2((held.pop(n) - tops[n]) * scale)
        totals[n] = 1.0 / jnp.sum(expo, 0, keepdims=True)
        weights[n] = expo.astype(jnp.bfloat16)

    def weighted(n):
        w, part = units[n]
        own = qkv[w * qlen : (w + 1) * qlen]
        values = jnp.concatenate([own[:, 2 * dim :][:, part], reg_values[:, part]], 0)
        mixed = dot(values, weights.pop(n), TN) * totals[n]
        done[n] = pick_heads(mixed, qlen, hdim)

    for n in range(len(units) + 8):
        if n < len(units):
            scores(n)
        if 0 <= n - 4 < len(units):
            exponentials(n - 4)
        if 0 <= n - 8:
            weighted(n - 8)
    per = dim // LANES
    return [
        jnp.concatenate([done[i * per + g] for g in range(per)], 0) for i in range(len(windows))
    ]


def register_attention(query, keys, values, hdim):
    dim = query.shape[1]
    mask = head_mask(REG, hdim)
    per = LANES // hdim
    scores = []
    for lo in range(0, dim, LANES):
        stacked = jnp.concatenate([query[:, lo : lo + LANES]] * per, 0) * mask
        scores.append(dot(keys[:, lo : lo + LANES], stacked, NT))
    scores = jnp.concatenate(scores, 1)
    top = jnp.max(scores, 0, keepdims=True)
    expo = jnp.exp2((scores - top) * (math.log2(math.e) / math.sqrt(hdim)))
    weights = (expo * (1.0 / jnp.sum(expo, 0, keepdims=True))).astype(jnp.bfloat16)
    mixed = dot(weights, values, TN)
    lane = lax.broadcasted_iota(jnp.int32, (REG, dim), 1) // hdim
    result = jnp.zeros((REG, dim), jnp.float32)
    for h in range(HEADS):
        result = jnp.where(lane == h, mixed[h * REG : (h + 1) * REG], result)
    return result.astype(jnp.bfloat16)


def block_kernel(
    x_hbm, reg_hbm, gain_hbm, gain_two_hbm, wqkv_hbm, wout_hbm,
    out_ref, reg_out_ref,
    x_ref, reg_ref, gain_ref, gain_two_ref, wqkv_ref, wout_ref, sems,
):
    pairs = [
        (x_hbm, x_ref), (reg_hbm, reg_ref), (gain_hbm, gain_ref),
        (wqkv_hbm, wqkv_ref), (wout_hbm, wout_ref), (gain_two_hbm, gain_two_ref),
    ]
    copies = [pltpu.make_async_copy(src, dst, sems.at[i]) for i, (src, dst) in enumerate(pairs)]
    for copy in copies:
        copy.start()
    for copy in copies[:3]:
        copy.wait()
    rows, width, dim = x_ref.shape
    hdim = dim // HEADS
    count = width // WIN
    gain = gain_ref[...]
    values = x_ref[...].astype(jnp.float32)
    tokens = jnp.concatenate(
        [values[:, w * WIN : (w + 1) * WIN, :].reshape(rows * WIN, dim) for w in range(count)], 0
    )
    normed = layer_norm(tokens, gain).astype(jnp.bfloat16)
    reg_normed = layer_norm(reg_ref[...], gain).astype(jnp.bfloat16)
    for copy in copies[3:]:
        copy.wait()
    qkv = dot(normed, wqkv_ref[...]).astype(jnp.bfloat16)
    reg_qkv = dot(reg_normed, wqkv_ref[...]).astype(jnp.bfloat16)
    reg_att = register_attention(
        reg_qkv[:, :dim],
        jnp.concatenate([qkv[:, dim : 2 * dim], reg_qkv[:, dim : 2 * dim]], 0),
        jnp.concatenate([qkv[:, 2 * dim :], reg_qkv[:, 2 * dim :]], 0),
        hdim,
    )
    reg_out = reg_ref[...] + dot(reg_att, wout_ref[...])
    reg_out_ref[...] = reg_out
    travelling = layer_norm(reg_out, gain_two_ref[...]).astype(jnp.bfloat16)
    for r in range(rows):
        out_ref[r, width:, :] = travelling
    qlen = rows * WIN
    mask = head_mask(qlen, hdim)
    reg_keys, reg_values = reg_qkv[:, dim : 2 * dim], reg_qkv[:, 2 * dim :]
    atts = attend_windows(
        qkv, reg_keys, reg_values, range(count), qlen, mask, hdim
    )
    att = jnp.concatenate([each.T.astype(jnp.bfloat16) for each in atts], 0)
    result = tokens + dot(att, wout_ref[...])
    for w in range(count):
        piece = result[w * qlen : (w + 1) * qlen].reshape(rows, WIN, dim)
        out_ref[:, w * WIN : (w + 1) * WIN, :] = piece.astype(jnp.bfloat16)


def grid_kernel(x_ref, gain_ref, wqkv_ref, wout_ref, out_ref, scratch):
    _, width, dim = out_ref.shape
    cls = width // WIN
    hdim = dim // HEADS
    qlen = WIN * WIN
    step = 4 if cls % 4 == 0 else 1
    gain = gain_ref[...]
    regs = jnp.concatenate([x_ref[a, width:, :] for a in range(WIN)], 0)
    reg_kv = dot(regs, wqkv_ref[:, dim:]).astype(jnp.bfloat16)
    mask = head_mask(qlen, hdim)
    lanes = [slice(g * LANES, (g + 1) * LANES) for g in range(dim // LANES)]
    for g, part in enumerate(lanes):
        for a in range(WIN):
            scratch[g, a * width : (a + 1) * width] = x_ref[a, :width, part].astype(jnp.float32)
    for first in range(0, cls, step):
        starts = [a * width + first + c for c in range(step) for a in range(WIN)]
        tokens = jnp.concatenate(
            [
                jnp.concatenate(
                    [scratch[g, pl.ds(start, WIN, stride=cls), :] for start in starts], 0
                )
                for g in range(len(lanes))
            ],
            1,
        )
        normed = layer_norm(tokens, gain).astype(jnp.bfloat16)
        qkv = dot(normed, wqkv_ref[...]).astype(jnp.bfloat16)
        atts = attend_windows(
            qkv, reg_kv[:, :dim], reg_kv[:, dim:], range(step), qlen, mask, hdim
        )
        att = jnp.concatenate([each.T.astype(jnp.bfloat16) for each in atts], 0)
        result = tokens + dot(att, wout_ref[...])
        for i, start in enumerate(starts):
            for g, part in enumerate(lanes):
                scratch[g, pl.ds(start, WIN, stride=cls), :] = result[i * WIN : (i + 1) * WIN, part]
    for g, part in enumerate(lanes):
        for a in range(WIN):
            out_ref[a, :, part] = scratch[g, a * width : (a + 1) * width].astype(jnp.bfloat16)


def call(kernel, outs, scratch=(), flops=0, in_specs=None):
    specs = {} if in_specs is None else {"in_specs": in_specs}
    return pl.pallas_call(
        kernel,
        out_shape=outs,
        scratch_shapes=list(scratch),
        compiler_params=pltpu.CompilerParams(vmem_limit_bytes=40 << 20),
        cost_estimate=pl.CostEstimate(flops=flops, bytes_accessed=4 << 20, transcendentals=0),
        **specs,
    )


def on_device(patches, registers, gain_one, gain_two, w_qkv_one, w_out_one, w_qkv_two, w_out_two):
    rows, width, dim = patches.shape
    nrow = lax.axis_size("row")
    per_band = nrow // WIN
    count = rows * width
    groups = [[a * per_band + p for a in ORDER] for p in range(per_band)]

    def exchange(values):
        return lax.all_to_all(
            values, "row", 0, 0, axis_index_groups=groups, tiled=True
        )

    bf16, f32 = jnp.bfloat16, jnp.float32
    shape = jax.ShapeDtypeStruct
    g_one, g_two = gain_one.reshape(1, dim), gain_two.reshape(1, dim)
    fetched = [
        pltpu.with_memory_space_constraint(value, pltpu.MemorySpace.HBM)
        for value in (patches, registers, g_one, g_two, w_qkv_one, w_out_one)
    ]
    outgoing, reg_out = call(
        block_kernel,
        (shape((rows, width + REG, dim), bf16), shape((REG, dim), f32)),
        [
            pltpu.VMEM((rows, width, dim), bf16),
            pltpu.VMEM((REG, dim), f32),
            pltpu.VMEM((1, dim), f32),
            pltpu.VMEM((1, dim), f32),
            pltpu.VMEM((dim, 3 * dim), bf16),
            pltpu.VMEM((dim, dim), bf16),
            pltpu.SemaphoreType.DMA((6,)),
        ],
        flops=2 * count * dim * 4 * dim,
        in_specs=[pl.BlockSpec(memory_space=pltpu.MemorySpace.HBM)] * 6,
    )(*fetched)
    finished = call(
        grid_kernel,
        shape((rows, width, dim), bf16),
        [
            pltpu.VMEM((dim // LANES, count, LANES), f32),
        ],
        flops=2 * count * dim * 6 * dim,
    )(exchange(outgoing), g_two, w_qkv_two, w_out_two)
    patches_out = exchange(finished)
    return (patches_out, reg_out)


def solution(mesh):
    in_specs = (
        P(("grp", "row"), None, None),
        P(("grp", "row"), None),
        P(),
        P(),
        P(),
        P(),
        P(),
        P(),
    )
    out_specs = (P(("grp", "row"), None, None), P(("grp", "row"), None))
    return jax.shard_map(
        on_device, mesh=mesh, in_specs=in_specs, out_specs=out_specs, check_vma=False
    )
```

```python
import functools
import math

import jax
import jax.numpy as jnp
from jax import lax
from jax.experimental import pallas as pl
from jax.experimental.pallas import tpu as pltpu
from jax.sharding import PartitionSpec as P

HEADS = 16
WIN = 8
REG = 16
LANES = 128
STAGE_AT = (0, 6, 10, 14)
BLOCK_GAPS, GRID_GAPS = (4, 8), (4, 8)
ORDER = (5, 4, 1, 0, 7, 6, 3, 2)

NT = (((1,), (1,)), ((), ()))
TN = (((0,), (0,)), ((), ()))
NN = (((1,), (0,)), ((), ()))


def dot(lhs, rhs, dims=NN):
    return lax.dot_general(lhs, rhs, dims, preferred_element_type=jnp.float32)


def layer_norm(values, gain):
    mean = jnp.mean(values, -1, keepdims=True)
    centred = values - mean
    spread = jnp.mean(centred * centred, -1, keepdims=True)
    return centred * lax.rsqrt(spread + 1e-05) * gain


def head_mask(qlen, hdim):
    per = LANES // hdim
    row = lax.broadcasted_iota(jnp.int32, (per * qlen, LANES), 0) // qlen
    lane = lax.broadcasted_iota(jnp.int32, (per * qlen, LANES), 1) // hdim
    return jnp.where(row == lane, 1.0, 0.0).astype(jnp.bfloat16)


def pick_heads(mixed, qlen, hdim):
    return jnp.concatenate(
        [
            mixed[h * hdim : (h + 1) * hdim, h * qlen : (h + 1) * qlen]
            for h in range(LANES // hdim)
        ],
        0,
    )


def attend_windows(qkv, reg_keys, reg_values, windows, qlen, mask, hdim, gaps, beside={}):
    dim = reg_keys.shape[1]
    units = [(w, slice(lo, lo + LANES)) for w in windows for lo in range(0, dim, LANES)]
    tops, totals, done, held, weights = {}, {}, {}, {}, {}

    def scores(n):
        w, part = units[n]
        own = qkv[w * qlen : (w + 1) * qlen]
        keys = jnp.concatenate([own[:, dim : 2 * dim][:, part], reg_keys[:, part]], 0)
        stacked = jnp.concatenate([own[:, part]] * (LANES // hdim), 0) * mask
        result = dot(keys, stacked, NT)
        held[n] = result
        tops[n] = jnp.max(result, 0, keepdims=True)

    def exponentials(n):
        scale = math.log2(math.e) / math.sqrt(hdim)
        expo = jnp.exp2((held.pop(n) - tops[n]) * scale)
        totals[n] = 1.0 / jnp.sum(expo, 0, keepdims=True)
        weights[n] = expo.astype(jnp.bfloat16)

    def weighted(n):
        w, part = units[n]
        own = qkv[w * qlen : (w + 1) * qlen]
        values = jnp.concatenate([own[:, 2 * dim :][:, part], reg_values[:, part]], 0)
        mixed = dot(values, weights.pop(n), TN) * totals[n]
        done[n] = pick_heads(mixed, qlen, hdim)

    to_expo, to_mixed = gaps
    for n in range(len(units) + to_mixed):
        if n < len(units):
            scores(n)
        if 0 <= n - to_expo < len(units):
            exponentials(n - to_expo)
        if 0 <= n - to_mixed:
            weighted(n - to_mixed)
        if n in beside:
            beside[n]()
    per = dim // LANES
    return [
        jnp.concatenate([done[i * per + g] for g in range(per)], 0) for i in range(len(windows))
    ]


def register_stages(query, keys, values, hdim, finish):
    dim = query.shape[1]
    held = {}

    def scores():
        mask = head_mask(REG, hdim)
        per = LANES // hdim
        parts = []
        for lo in range(0, dim, LANES):
            stacked = jnp.concatenate([query[:, lo : lo + LANES]] * per, 0) * mask
            parts.append(dot(keys[:, lo : lo + LANES], stacked, NT))
        held["scores"] = jnp.concatenate(parts, 1)

    def weights():
        top = jnp.max(held["scores"], 0, keepdims=True)
        scale = math.log2(math.e) / math.sqrt(hdim)
        expo = jnp.exp2((held.pop("scores") - top) * scale)
        held["weights"] = (expo * (1.0 / jnp.sum(expo, 0, keepdims=True))).astype(jnp.bfloat16)

    def mixed():
        result = dot(held.pop("weights"), values, TN)
        lane = lax.broadcasted_iota(jnp.int32, (REG, dim), 1) // hdim
        picked = jnp.zeros((REG, dim), jnp.float32)
        for h in range(HEADS):
            picked = jnp.where(lane == h, result[h * REG : (h + 1) * REG], picked)
        held["picked"] = picked.astype(jnp.bfloat16)

    return [scores, weights, mixed, lambda: finish(held["picked"])]


def block_kernel(
    x_hbm, reg_hbm, gain_hbm, gain_two_hbm, wqkv_hbm, wout_hbm,
    out_ref, reg_out_hbm,
    reg_out_ref, x_ref, reg_ref, gain_ref, gain_two_ref, wqkv_ref, wout_ref, sems,
):
    dim = x_ref.shape[2]
    thirds = [slice(j * dim, (j + 1) * dim) for j in range(3)]
    pairs = [
        (x_hbm, x_ref), (reg_hbm, reg_ref), (gain_hbm, gain_ref),
        *((wqkv_hbm.at[:, part], wqkv_ref.at[:, part]) for part in thirds),
        (wout_hbm, wout_ref), (gain_two_hbm, gain_two_ref),
    ]
    copies = [pltpu.make_async_copy(src, dst, sems.at[i]) for i, (src, dst) in enumerate(pairs)]
    for copy in copies:
        copy.start()
    for copy in copies[:3]:
        copy.wait()
    rows, width, dim = x_ref.shape
    hdim = dim // HEADS
    count = width // WIN
    gain = gain_ref[...]
    values = x_ref[...].astype(jnp.float32)
    tokens = jnp.concatenate(
        [values[:, w * WIN : (w + 1) * WIN, :].reshape(rows * WIN, dim) for w in range(count)], 0
    )
    normed = layer_norm(tokens, gain).astype(jnp.bfloat16)
    reg_normed = layer_norm(reg_ref[...], gain).astype(jnp.bfloat16)
    both = []
    everything = jnp.concatenate([normed, reg_normed], 0)
    for part, copy in zip(thirds, copies[3:6]):
        copy.wait()
        both.append(dot(everything, wqkv_ref[:, part]).astype(jnp.bfloat16))
    both = jnp.concatenate(both, 1)
    qkv, reg_qkv = both[: rows * width], both[rows * width :]
    for copy in copies[6:]:
        copy.wait()

    leaving = pltpu.make_async_copy(reg_out_ref, reg_out_hbm, sems.at[8])

    def finish(reg_att):
        reg_out = reg_ref[...] + dot(reg_att, wout_ref[...])
        reg_out_ref[...] = reg_out
        leaving.start()
        travelling = layer_norm(reg_out, gain_two_ref[...]).astype(jnp.bfloat16)
        for r in range(rows):
            out_ref[r, width:, :] = travelling

    stages = register_stages(
        reg_qkv[:, :dim],
        jnp.concatenate([qkv[:, dim : 2 * dim], reg_qkv[:, dim : 2 * dim]], 0),
        jnp.concatenate([qkv[:, 2 * dim :], reg_qkv[:, 2 * dim :]], 0),
        hdim,
        finish,
    )
    qlen = rows * WIN
    mask = head_mask(qlen, hdim)
    reg_keys, reg_values = reg_qkv[:, dim : 2 * dim], reg_qkv[:, 2 * dim :]
    atts = attend_windows(
        qkv, reg_keys, reg_values, range(count), qlen, mask, hdim, BLOCK_GAPS, dict(zip(STAGE_AT, stages))
    )
    att = jnp.concatenate([each.T.astype(jnp.bfloat16) for each in atts], 0)
    result = tokens + dot(att, wout_ref[...])
    for w in range(count):
        piece = result[w * qlen : (w + 1) * qlen].reshape(rows, WIN, dim)
        out_ref[:, w * WIN : (w + 1) * WIN, :] = piece.astype(jnp.bfloat16)
    leaving.wait()


def grid_kernel(x_ref, gain_ref, wqkv_ref, wout_ref, out_ref, scratch):
    _, width, dim = out_ref.shape
    cls = width // WIN
    hdim = dim // HEADS
    qlen = WIN * WIN
    step = 4 if cls % 4 == 0 else 1
    gain = gain_ref[...]
    regs = jnp.concatenate([x_ref[a, width:, :] for a in range(WIN)], 0)
    reg_kv = dot(regs, wqkv_ref[:, dim:]).astype(jnp.bfloat16)
    mask = head_mask(qlen, hdim)
    lanes = [slice(g * LANES, (g + 1) * LANES) for g in range(dim // LANES)]
    for g, part in enumerate(lanes):
        for a in range(WIN):
            scratch[g, a * width : (a + 1) * width] = x_ref[a, :width, part].astype(jnp.float32)
    for first in range(0, cls, step):
        starts = [a * width + first + c for c in range(step) for a in range(WIN)]
        tokens = jnp.concatenate(
            [
                jnp.concatenate(
                    [scratch[g, pl.ds(start, WIN, stride=cls), :] for start in starts], 0
                )
                for g in range(len(lanes))
            ],
            1,
        )
        normed = layer_norm(tokens, gain).astype(jnp.bfloat16)
        qkv = dot(normed, wqkv_ref[...]).astype(jnp.bfloat16)
        atts = attend_windows(
            qkv, reg_kv[:, :dim], reg_kv[:, dim:], range(step), qlen, mask, hdim, GRID_GAPS
        )
        att = jnp.concatenate([each.T.astype(jnp.bfloat16) for each in atts], 0)
        result = tokens + dot(att, wout_ref[...])
        for i, start in enumerate(starts):
            for g, part in enumerate(lanes):
                scratch[g, pl.ds(start, WIN, stride=cls), :] = result[i * WIN : (i + 1) * WIN, part]
    for g, part in enumerate(lanes):
        for a in range(WIN):
            out_ref[a, :, part] = scratch[g, a * width : (a + 1) * width].astype(jnp.bfloat16)


def call(kernel, outs, scratch=(), flops=0, **specs):
    return pl.pallas_call(
        kernel,
        out_shape=outs,
        scratch_shapes=list(scratch),
        compiler_params=pltpu.CompilerParams(vmem_limit_bytes=40 << 20),
        cost_estimate=pl.CostEstimate(flops=flops, bytes_accessed=4 << 20, transcendentals=0),
        **specs,
    )


def on_device(patches, registers, gain_one, gain_two, w_qkv_one, w_out_one, w_qkv_two, w_out_two):
    rows, width, dim = patches.shape
    nrow = lax.axis_size("row")
    per_band = nrow // WIN
    count = rows * width
    groups = [[a * per_band + p for a in ORDER] for p in range(per_band)]

    def exchange(values):
        return lax.all_to_all(
            values, "row", 0, 0, axis_index_groups=groups, tiled=True
        )

    bf16, f32 = jnp.bfloat16, jnp.float32
    shape = jax.ShapeDtypeStruct
    g_one, g_two = gain_one.reshape(1, dim), gain_two.reshape(1, dim)
    fetched = [
        pltpu.with_memory_space_constraint(value, pltpu.MemorySpace.HBM)
        for value in (patches, registers, g_one, g_two, w_qkv_one, w_out_one)
    ]
    outgoing, reg_out = call(
        block_kernel,
        (shape((rows, width + REG, dim), bf16), shape((REG, dim), f32)),
        [
            pltpu.VMEM((REG, dim), f32),
            pltpu.VMEM((rows, width, dim), bf16),
            pltpu.VMEM((REG, dim), f32),
            pltpu.VMEM((1, dim), f32),
            pltpu.VMEM((1, dim), f32),
            pltpu.VMEM((dim, 3 * dim), bf16),
            pltpu.VMEM((dim, dim), bf16),
            pltpu.SemaphoreType.DMA((9,)),
        ],
        flops=2 * count * dim * 4 * dim,
        in_specs=[pl.BlockSpec(memory_space=pltpu.MemorySpace.HBM)] * 6,
        out_specs=(
            pl.BlockSpec(memory_space=pltpu.MemorySpace.VMEM),
            pl.BlockSpec(memory_space=pltpu.MemorySpace.HBM),
        ),
    )(*fetched)
    finished = call(
        grid_kernel,
        shape((rows, width, dim), bf16),
        [
            pltpu.VMEM((dim // LANES, count, LANES), f32),
        ],
        flops=2 * count * dim * 6 * dim,
    )(exchange(outgoing), g_two, w_qkv_two, w_out_two)
    patches_out = exchange(finished)
    return (patches_out, reg_out)


def solution(mesh):
    in_specs = (
        P(("grp", "row"), None, None),
        P(("grp", "row"), None),
        P(),
        P(),
        P(),
        P(),
        P(),
        P(),
    )
    out_specs = (P(("grp", "row"), None, None), P(("grp", "row"), None))
    return jax.shard_map(
        on_device, mesh=mesh, in_specs=in_specs, out_specs=out_specs, check_vma=False
    )
```

```python
import functools
import math

import jax
import jax.numpy as jnp
from jax import lax
from jax.experimental import pallas as pl
from jax.experimental.pallas import tpu as pltpu
from jax.sharding import PartitionSpec as P

HEADS = 16
WIN = 8
REG = 16
LANES = 128
STAGE_AT = (0, 10, 16, 20)
BLOCK_GAPS, GRID_GAPS = (4, 8), (5, 10)
ORDER = (5, 4, 1, 0, 7, 6, 3, 2)

NT = (((1,), (1,)), ((), ()))
TN = (((0,), (0,)), ((), ()))
NN = (((1,), (0,)), ((), ()))


def dot(lhs, rhs, dims=NN):
    return lax.dot_general(lhs, rhs, dims, preferred_element_type=jnp.float32)


def layer_norm(values, gain):
    mean = jnp.mean(values, -1, keepdims=True)
    centred = values - mean
    spread = jnp.mean(centred * centred, -1, keepdims=True)
    return centred * lax.rsqrt(spread + 1e-05) * gain


def score_scale(hdim):
    return math.log2(math.e) / math.sqrt(hdim)


def head_mask(qlen, hdim):
    per = LANES // hdim
    row = lax.broadcasted_iota(jnp.int32, (per * qlen, LANES), 0) // qlen
    lane = lax.broadcasted_iota(jnp.int32, (per * qlen, LANES), 1) // hdim
    return jnp.where(row == lane, 1.0, 0.0).astype(jnp.bfloat16)


def pick_heads(mixed, qlen, hdim):
    return jnp.concatenate(
        [
            mixed[h * hdim : (h + 1) * hdim, h * qlen : (h + 1) * qlen]
            for h in range(LANES // hdim)
        ],
        0,
    )


def attend_windows(qkv, reg_keys, reg_values, windows, qlen, mask, hdim, gaps, beside={}):
    dim = reg_keys.shape[1]
    units = [(w, slice(lo, lo + LANES)) for w in windows for lo in range(0, dim, LANES)]
    tops, totals, done, held, weights = {}, {}, {}, {}, {}

    def scores(n):
        w, part = units[n]
        own = qkv[w * qlen : (w + 1) * qlen]
        keys = jnp.concatenate([own[:, dim : 2 * dim][:, part], reg_keys[:, part]], 0)
        stacked = jnp.concatenate([own[:, part]] * (LANES // hdim), 0) * mask
        result = dot(keys, stacked, NT)
        held[n] = result
        tops[n] = jnp.max(result, 0, keepdims=True)

    def exponentials(n):
        expo = jnp.exp2(held.pop(n) - tops[n])
        totals[n] = 1.0 / jnp.sum(expo, 0, keepdims=True)
        weights[n] = expo.astype(jnp.bfloat16)

    def weighted(n):
        w, part = units[n]
        own = qkv[w * qlen : (w + 1) * qlen]
        values = jnp.concatenate([own[:, 2 * dim :][:, part], reg_values[:, part]], 0)
        mixed = dot(values, weights.pop(n), TN) * totals[n]
        done[n] = pick_heads(mixed, qlen, hdim)

    to_expo, to_mixed = gaps
    for n in range(len(units) + to_mixed):
        if n < len(units):
            scores(n)
        if 0 <= n - to_expo < len(units):
            exponentials(n - to_expo)
        if 0 <= n - to_mixed:
            weighted(n - to_mixed)
        if n in beside:
            beside[n]()
    per = dim // LANES
    return [
        jnp.concatenate([done[i * per + g] for g in range(per)], 0) for i in range(len(windows))
    ]


def register_stages(query, keys, values, hdim, finish):
    dim = query.shape[1]
    held = {}

    def scores():
        mask = head_mask(REG, hdim)
        per = LANES // hdim
        parts = []
        for lo in range(0, dim, LANES):
            stacked = jnp.concatenate([query[:, lo : lo + LANES]] * per, 0) * mask
            parts.append(dot(keys[:, lo : lo + LANES], stacked, NT))
        held["scores"] = jnp.concatenate(parts, 1)

    def weights():
        top = jnp.max(held["scores"], 0, keepdims=True)
        expo = jnp.exp2(held.pop("scores") - top)
        held["weights"] = (expo * (1.0 / jnp.sum(expo, 0, keepdims=True))).astype(jnp.bfloat16)

    def mixed():
        result = dot(held.pop("weights"), values, TN)
        lane = lax.broadcasted_iota(jnp.int32, (REG, dim), 1) // hdim
        picked = jnp.zeros((REG, dim), jnp.float32)
        for h in range(HEADS):
            picked = jnp.where(lane == h, result[h * REG : (h + 1) * REG], picked)
        held["picked"] = picked.astype(jnp.bfloat16)

    return [scores, weights, mixed, lambda: finish(held["picked"])]


def block_kernel(
    x_hbm, reg_hbm, gain_hbm, gain_two_hbm, wqkv_hbm, wout_hbm,
    out_ref, reg_out_hbm,
    reg_out_ref, x_ref, reg_ref, gain_ref, gain_two_ref, wqkv_ref, wout_ref, sems,
):
    dim = x_ref.shape[2]
    parts = [slice(0, 2 * dim), slice(2 * dim, 3 * dim)]
    pairs = [
        (x_hbm, x_ref), (reg_hbm, reg_ref), (gain_hbm, gain_ref),
        *((wqkv_hbm.at[:, part], wqkv_ref.at[:, part]) for part in parts),
        (wout_hbm, wout_ref), (gain_two_hbm, gain_two_ref),
    ]
    copies = [pltpu.make_async_copy(src, dst, sems.at[i]) for i, (src, dst) in enumerate(pairs)]
    for copy in copies:
        copy.start()
    for copy in copies[:3]:
        copy.wait()
    rows, width, dim = x_ref.shape
    hdim = dim // HEADS
    count = width // WIN
    gain = gain_ref[...]
    values = x_ref[...].astype(jnp.float32)
    tokens = jnp.concatenate(
        [values[:, w * WIN : (w + 1) * WIN, :].reshape(rows * WIN, dim) for w in range(count)], 0
    )
    normed = layer_norm(tokens, gain).astype(jnp.bfloat16)
    reg_normed = layer_norm(reg_ref[...], gain).astype(jnp.bfloat16)
    everything = jnp.concatenate([normed, reg_normed], 0)
    copies[3].wait()
    early = dot(everything, wqkv_ref[:, parts[0]])
    early = jnp.concatenate([early[:, :dim] * score_scale(hdim), early[:, dim:]], 1)
    for copy in copies[4:]:
        copy.wait()
    late = dot(everything, wqkv_ref[:, parts[1]])
    both = jnp.concatenate([early.astype(jnp.bfloat16), late.astype(jnp.bfloat16)], 1)
    qkv, reg_qkv = both[: rows * width], both[rows * width :]

    leaving = pltpu.make_async_copy(reg_out_ref, reg_out_hbm, sems.at[7])

    def finish(reg_att):
        reg_out = reg_ref[...] + dot(reg_att, wout_ref[...])
        reg_out_ref[...] = reg_out
        leaving.start()
        travelling = layer_norm(reg_out, gain_two_ref[...]).astype(jnp.bfloat16)
        for r in range(rows):
            out_ref[r, width:, :] = travelling

    stages = register_stages(
        reg_qkv[:, :dim],
        jnp.concatenate([qkv[:, dim : 2 * dim], reg_qkv[:, dim : 2 * dim]], 0),
        jnp.concatenate([qkv[:, 2 * dim :], reg_qkv[:, 2 * dim :]], 0),
        hdim,
        finish,
    )
    qlen = rows * WIN
    mask = head_mask(qlen, hdim)
    reg_keys, reg_values = reg_qkv[:, dim : 2 * dim], reg_qkv[:, 2 * dim :]
    atts = attend_windows(
        qkv, reg_keys, reg_values, range(count), qlen, mask, hdim, BLOCK_GAPS, dict(zip(STAGE_AT, stages))
    )
    att = jnp.concatenate([each.T.astype(jnp.bfloat16) for each in atts], 0)
    result = tokens + dot(att, wout_ref[...])
    for w in range(count):
        piece = result[w * qlen : (w + 1) * qlen].reshape(rows, WIN, dim)
        out_ref[:, w * WIN : (w + 1) * WIN, :] = piece.astype(jnp.bfloat16)
    leaving.wait()


def grid_kernel(x_ref, gain_ref, wqkv_ref, wout_ref, out_ref, scratch):
    _, width, dim = out_ref.shape
    cls = width // WIN
    hdim = dim // HEADS
    qlen = WIN * WIN
    step = 4 if cls % 4 == 0 else 1
    gain = gain_ref[...]
    regs = jnp.concatenate([x_ref[a, width:, :] for a in range(WIN)], 0)
    reg_kv = dot(regs, wqkv_ref[:, dim:]).astype(jnp.bfloat16)
    mask = head_mask(qlen, hdim)
    lanes = [slice(g * LANES, (g + 1) * LANES) for g in range(dim // LANES)]
    for g, part in enumerate(lanes):
        for a in range(WIN):
            scratch[g, a * width : (a + 1) * width] = x_ref[a, :width, part].astype(jnp.float32)
    for first in range(0, cls, step):
        starts = [a * width + first + c for c in range(step) for a in range(WIN)]
        tokens = jnp.concatenate(
            [
                jnp.concatenate(
                    [scratch[g, pl.ds(start, WIN, stride=cls), :] for start in starts], 0
                )
                for g in range(len(lanes))
            ],
            1,
        )
        normed = layer_norm(tokens, gain).astype(jnp.bfloat16)
        qkv = jnp.concatenate(
            [
                (dot(normed, wqkv_ref[:, :dim]) * score_scale(hdim)).astype(jnp.bfloat16),
                dot(normed, wqkv_ref[:, dim:]).astype(jnp.bfloat16),
            ],
            1,
        )
        atts = attend_windows(
            qkv, reg_kv[:, :dim], reg_kv[:, dim:], range(step), qlen, mask, hdim, GRID_GAPS
        )
        att = jnp.concatenate([each.T.astype(jnp.bfloat16) for each in atts], 0)
        result = tokens + dot(att, wout_ref[...])
        for i, start in enumerate(starts):
            for g, part in enumerate(lanes):
                scratch[g, pl.ds(start, WIN, stride=cls), :] = result[i * WIN : (i + 1) * WIN, part]
    for g, part in enumerate(lanes):
        for a in range(WIN):
            out_ref[a, :, part] = scratch[g, a * width : (a + 1) * width].astype(jnp.bfloat16)


def call(kernel, outs, scratch=(), flops=0, **specs):
    return pl.pallas_call(
        kernel,
        out_shape=outs,
        scratch_shapes=list(scratch),
        compiler_params=pltpu.CompilerParams(vmem_limit_bytes=40 << 20),
        cost_estimate=pl.CostEstimate(flops=flops, bytes_accessed=4 << 20, transcendentals=0),
        **specs,
    )


def on_device(patches, registers, gain_one, gain_two, w_qkv_one, w_out_one, w_qkv_two, w_out_two):
    rows, width, dim = patches.shape
    nrow = lax.axis_size("row")
    per_band = nrow // WIN
    count = rows * width
    groups = [[a * per_band + p for a in ORDER] for p in range(per_band)]

    def exchange(values):
        return lax.all_to_all(
            values, "row", 0, 0, axis_index_groups=groups, tiled=True
        )

    bf16, f32 = jnp.bfloat16, jnp.float32
    shape = jax.ShapeDtypeStruct
    g_one, g_two = gain_one.reshape(1, dim), gain_two.reshape(1, dim)
    fetched = [
        pltpu.with_memory_space_constraint(value, pltpu.MemorySpace.HBM)
        for value in (patches, registers, g_one, g_two, w_qkv_one, w_out_one)
    ]
    outgoing, reg_out = call(
        block_kernel,
        (shape((rows, width + REG, dim), bf16), shape((REG, dim), f32)),
        [
            pltpu.VMEM((REG, dim), f32),
            pltpu.VMEM((rows, width, dim), bf16),
            pltpu.VMEM((REG, dim), f32),
            pltpu.VMEM((1, dim), f32),
            pltpu.VMEM((1, dim), f32),
            pltpu.VMEM((dim, 3 * dim), bf16),
            pltpu.VMEM((dim, dim), bf16),
            pltpu.SemaphoreType.DMA((8,)),
        ],
        flops=2 * count * dim * 4 * dim,
        in_specs=[pl.BlockSpec(memory_space=pltpu.MemorySpace.HBM)] * 6,
        out_specs=(
            pl.BlockSpec(memory_space=pltpu.MemorySpace.VMEM),
            pl.BlockSpec(memory_space=pltpu.MemorySpace.HBM),
        ),
    )(*fetched)
    finished = call(
        grid_kernel,
        shape((rows, width, dim), bf16),
        [
            pltpu.VMEM((dim // LANES, count, LANES), f32),
        ],
        flops=2 * count * dim * 6 * dim,
    )(exchange(outgoing), g_two, w_qkv_two, w_out_two)
    patches_out = exchange(finished)
    return (patches_out, reg_out)


def solution(mesh):
    in_specs = (
        P(("grp", "row"), None, None),
        P(("grp", "row"), None),
        P(),
        P(),
        P(),
        P(),
        P(),
        P(),
    )
    out_specs = (P(("grp", "row"), None, None), P(("grp", "row"), None))
    return jax.shard_map(
        on_device, mesh=mesh, in_specs=in_specs, out_specs=out_specs, check_vma=False
    )
```

```python
import functools
import math

import jax
import jax.numpy as jnp
from jax import lax
from jax.experimental import pallas as pl
from jax.experimental.pallas import tpu as pltpu
from jax.sharding import PartitionSpec as P

HEADS = 16
WIN = 8
REG = 16
LANES = 128
STAGE_AT = (0, 10, 16, 20)
BLOCK_GAPS, GRID_GAPS = (4, 8), (5, 10)
ORDER = (5, 4, 3, 0, 7, 6, 1, 2)

NT = (((1,), (1,)), ((), ()))
TN = (((0,), (0,)), ((), ()))
NN = (((1,), (0,)), ((), ()))


def dot(lhs, rhs, dims=NN):
    return lax.dot_general(lhs, rhs, dims, preferred_element_type=jnp.float32)


def layer_norm(values, gain):
    mean = jnp.mean(values, -1, keepdims=True)
    centred = values - mean
    spread = jnp.mean(centred * centred, -1, keepdims=True)
    return centred * lax.rsqrt(spread + 1e-05) * gain


def score_scale(hdim):
    return math.log2(math.e) / math.sqrt(hdim)


def head_mask(qlen, hdim):
    per = LANES // hdim
    row = lax.broadcasted_iota(jnp.int32, (per * qlen, LANES), 0) // qlen
    lane = lax.broadcasted_iota(jnp.int32, (per * qlen, LANES), 1) // hdim
    return jnp.where(row == lane, 1.0, 0.0).astype(jnp.bfloat16)


def pick_heads(mixed, qlen, hdim):
    return jnp.concatenate(
        [
            mixed[h * hdim : (h + 1) * hdim, h * qlen : (h + 1) * qlen]
            for h in range(LANES // hdim)
        ],
        0,
    )


def attend_windows(qkv, reg_keys, reg_values, windows, qlen, mask, hdim, gaps, beside={}):
    dim = reg_keys.shape[1]
    units = [(w, slice(lo, lo + LANES)) for w in windows for lo in range(0, dim, LANES)]
    tops, totals, done, held, weights = {}, {}, {}, {}, {}

    def scores(n):
        w, part = units[n]
        own = qkv[w * qlen : (w + 1) * qlen]
        keys = jnp.concatenate([own[:, dim : 2 * dim][:, part], reg_keys[:, part]], 0)
        stacked = jnp.concatenate([own[:, part]] * (LANES // hdim), 0) * mask
        result = dot(keys, stacked, NT)
        held[n] = result
        tops[n] = jnp.max(result, 0, keepdims=True)

    def exponentials(n):
        expo = jnp.exp2(held.pop(n) - tops[n])
        totals[n] = 1.0 / jnp.sum(expo, 0, keepdims=True)
        weights[n] = expo.astype(jnp.bfloat16)

    def weighted(n):
        w, part = units[n]
        own = qkv[w * qlen : (w + 1) * qlen]
        values = jnp.concatenate([own[:, 2 * dim :][:, part], reg_values[:, part]], 0)
        mixed = dot(values, weights.pop(n), TN) * totals[n]
        done[n] = pick_heads(mixed, qlen, hdim)

    to_expo, to_mixed = gaps
    for n in range(len(units) + to_mixed):
        if n < len(units):
            scores(n)
        if 0 <= n - to_expo < len(units):
            exponentials(n - to_expo)
        if 0 <= n - to_mixed:
            weighted(n - to_mixed)
        if n in beside:
            beside[n]()
    per = dim // LANES
    return [
        jnp.concatenate([done[i * per + g] for g in range(per)], 0) for i in range(len(windows))
    ]


def register_stages(query, keys, values, hdim, finish):
    dim = query.shape[1]
    held = {}

    def scores():
        mask = head_mask(REG, hdim)
        per = LANES // hdim
        parts = []
        for lo in range(0, dim, LANES):
            stacked = jnp.concatenate([query[:, lo : lo + LANES]] * per, 0) * mask
            parts.append(dot(keys[:, lo : lo + LANES], stacked, NT))
        held["scores"] = jnp.concatenate(parts, 1)

    def weights():
        top = jnp.max(held["scores"], 0, keepdims=True)
        expo = jnp.exp2(held.pop("scores") - top)
        held["weights"] = (expo * (1.0 / jnp.sum(expo, 0, keepdims=True))).astype(jnp.bfloat16)

    def mixed():
        result = dot(held.pop("weights"), values, TN)
        lane = lax.broadcasted_iota(jnp.int32, (REG, dim), 1) // hdim
        picked = jnp.zeros((REG, dim), jnp.float32)
        for h in range(HEADS):
            picked = jnp.where(lane == h, result[h * REG : (h + 1) * REG], picked)
        held["picked"] = picked.astype(jnp.bfloat16)

    return [scores, weights, mixed, lambda: finish(held["picked"])]


def block_kernel(
    x_hbm, reg_hbm, gain_hbm, gain_two_hbm, wqkv_hbm, wout_hbm,
    out_ref, reg_out_hbm,
    reg_out_ref, x_ref, reg_ref, gain_ref, gain_two_ref, wqkv_ref, wout_ref, sems,
):
    dim = x_ref.shape[2]
    parts = [slice(0, 2 * dim), slice(2 * dim, 3 * dim)]
    pairs = [
        (x_hbm, x_ref), (reg_hbm, reg_ref), (gain_hbm, gain_ref),
        *((wqkv_hbm.at[:, part], wqkv_ref.at[:, part]) for part in parts),
        (wout_hbm, wout_ref), (gain_two_hbm, gain_two_ref),
    ]
    copies = [pltpu.make_async_copy(src, dst, sems.at[i]) for i, (src, dst) in enumerate(pairs)]
    for copy in copies:
        copy.start()
    for copy in copies[:3]:
        copy.wait()
    rows, width, dim = x_ref.shape
    hdim = dim // HEADS
    count = width // WIN
    gain = gain_ref[...]
    values = x_ref[...].astype(jnp.float32)
    tokens = jnp.concatenate(
        [values[:, w * WIN : (w + 1) * WIN, :].reshape(rows * WIN, dim) for w in range(count)], 0
    )
    normed = layer_norm(tokens, gain).astype(jnp.bfloat16)
    reg_normed = layer_norm(reg_ref[...], gain).astype(jnp.bfloat16)
    everything = jnp.concatenate([normed, reg_normed], 0)
    copies[3].wait()
    early = dot(everything, wqkv_ref[:, parts[0]])
    early = jnp.concatenate([early[:, :dim] * score_scale(hdim), early[:, dim:]], 1)
    for copy in copies[4:]:
        copy.wait()
    late = dot(everything, wqkv_ref[:, parts[1]])
    both = jnp.concatenate([early.astype(jnp.bfloat16), late.astype(jnp.bfloat16)], 1)
    qkv, reg_qkv = both[: rows * width], both[rows * width :]

    leaving = pltpu.make_async_copy(reg_out_ref, reg_out_hbm, sems.at[7])

    def finish(reg_att):
        reg_out = reg_ref[...] + dot(reg_att, wout_ref[...])
        reg_out_ref[...] = reg_out
        leaving.start()
        travelling = layer_norm(reg_out, gain_two_ref[...]).astype(jnp.bfloat16)
        for r in range(rows):
            out_ref[r, width:, :] = travelling

    stages = register_stages(
        reg_qkv[:, :dim],
        jnp.concatenate([qkv[:, dim : 2 * dim], reg_qkv[:, dim : 2 * dim]], 0),
        jnp.concatenate([qkv[:, 2 * dim :], reg_qkv[:, 2 * dim :]], 0),
        hdim,
        finish,
    )
    qlen = rows * WIN
    mask = head_mask(qlen, hdim)
    reg_keys, reg_values = reg_qkv[:, dim : 2 * dim], reg_qkv[:, 2 * dim :]
    atts = attend_windows(
        qkv, reg_keys, reg_values, range(count), qlen, mask, hdim, BLOCK_GAPS, dict(zip(STAGE_AT, stages))
    )
    att = jnp.concatenate([each.T.astype(jnp.bfloat16) for each in atts], 0)
    result = tokens + dot(att, wout_ref[...])
    for w in range(count):
        piece = result[w * qlen : (w + 1) * qlen].reshape(rows, WIN, dim)
        out_ref[:, w * WIN : (w + 1) * WIN, :] = piece.astype(jnp.bfloat16)
    leaving.wait()


def grid_kernel(x_ref, gain_ref, wqkv_ref, wout_ref, out_ref, scratch):
    _, width, dim = out_ref.shape
    cls = width // WIN
    hdim = dim // HEADS
    qlen = WIN * WIN
    step = 4 if cls % 4 == 0 else 1
    gain = gain_ref[...]
    regs = jnp.concatenate([x_ref[a, width:, :] for a in range(WIN)], 0)
    reg_kv = dot(regs, wqkv_ref[:, dim:]).astype(jnp.bfloat16)
    mask = head_mask(qlen, hdim)
    lanes = [slice(g * LANES, (g + 1) * LANES) for g in range(dim // LANES)]
    for g, part in enumerate(lanes):
        for a in range(WIN):
            scratch[g, a * width : (a + 1) * width] = x_ref[a, :width, part].astype(jnp.float32)
    for first in range(0, cls, step):
        starts = [a * width + first + c for c in range(step) for a in range(WIN)]
        tokens = jnp.concatenate(
            [
                jnp.concatenate(
                    [scratch[g, pl.ds(start, WIN, stride=cls), :] for start in starts], 0
                )
                for g in range(len(lanes))
            ],
            1,
        )
        normed = layer_norm(tokens, gain).astype(jnp.bfloat16)
        qkv = jnp.concatenate(
            [
                (dot(normed, wqkv_ref[:, :dim]) * score_scale(hdim)).astype(jnp.bfloat16),
                dot(normed, wqkv_ref[:, dim:]).astype(jnp.bfloat16),
            ],
            1,
        )
        atts = attend_windows(
            qkv, reg_kv[:, :dim], reg_kv[:, dim:], range(step), qlen, mask, hdim, GRID_GAPS
        )
        att = jnp.concatenate([each.T.astype(jnp.bfloat16) for each in atts], 0)
        result = tokens + dot(att, wout_ref[...])
        for i, start in enumerate(starts):
            for g, part in enumerate(lanes):
                scratch[g, pl.ds(start, WIN, stride=cls), :] = result[i * WIN : (i + 1) * WIN, part]
    for g, part in enumerate(lanes):
        for a in range(WIN):
            out_ref[a, :, part] = scratch[g, a * width : (a + 1) * width].astype(jnp.bfloat16)


def call(kernel, outs, scratch=(), flops=0, **specs):
    return pl.pallas_call(
        kernel,
        out_shape=outs,
        scratch_shapes=list(scratch),
        compiler_params=pltpu.CompilerParams(vmem_limit_bytes=40 << 20),
        cost_estimate=pl.CostEstimate(flops=flops, bytes_accessed=4 << 20, transcendentals=0),
        **specs,
    )


def on_device(patches, registers, gain_one, gain_two, w_qkv_one, w_out_one, w_qkv_two, w_out_two):
    rows, width, dim = patches.shape
    nrow = lax.axis_size("row")
    per_band = nrow // WIN
    count = rows * width
    groups = [[a * per_band + p for a in ORDER] for p in range(per_band)]

    def exchange(values):
        return lax.all_to_all(
            values, "row", 0, 0, axis_index_groups=groups, tiled=True
        )

    bf16, f32 = jnp.bfloat16, jnp.float32
    shape = jax.ShapeDtypeStruct
    g_one, g_two = gain_one.reshape(1, dim), gain_two.reshape(1, dim)
    fetched = [
        pltpu.with_memory_space_constraint(value, pltpu.MemorySpace.HBM)
        for value in (patches, registers, g_one, g_two, w_qkv_one, w_out_one)
    ]
    outgoing, reg_out = call(
        block_kernel,
        (shape((rows, width + REG, dim), bf16), shape((REG, dim), f32)),
        [
            pltpu.VMEM((REG, dim), f32),
            pltpu.VMEM((rows, width, dim), bf16),
            pltpu.VMEM((REG, dim), f32),
            pltpu.VMEM((1, dim), f32),
            pltpu.VMEM((1, dim), f32),
            pltpu.VMEM((dim, 3 * dim), bf16),
            pltpu.VMEM((dim, dim), bf16),
            pltpu.SemaphoreType.DMA((8,)),
        ],
        flops=2 * count * dim * 4 * dim,
        in_specs=[pl.BlockSpec(memory_space=pltpu.MemorySpace.HBM)] * 6,
        out_specs=(
            pl.BlockSpec(memory_space=pltpu.MemorySpace.VMEM),
            pl.BlockSpec(memory_space=pltpu.MemorySpace.HBM),
        ),
    )(*fetched)
    finished = call(
        grid_kernel,
        shape((rows, width, dim), bf16),
        [
            pltpu.VMEM((dim // LANES, count, LANES), f32),
        ],
        flops=2 * count * dim * 6 * dim,
    )(exchange(outgoing), g_two, w_qkv_two, w_out_two)
    patches_out = exchange(finished)
    return (patches_out, reg_out)


def solution(mesh):
    in_specs = (
        P(("grp", "row"), None, None),
        P(("grp", "row"), None),
        P(),
        P(),
        P(),
        P(),
        P(),
        P(),
    )
    out_specs = (P(("grp", "row"), None, None), P(("grp", "row"), None))
    return jax.shard_map(
        on_device, mesh=mesh, in_specs=in_specs, out_specs=out_specs, check_vma=False
    )
```

```python
import functools
import math

import jax
import jax.numpy as jnp
from jax import lax
from jax.experimental import pallas as pl
from jax.experimental.pallas import tpu as pltpu
from jax.sharding import PartitionSpec as P

HEADS = 16
WIN = 8
REG = 16
LANES = 128
STAGE_AT = (0, 8, 14, 18)
BLOCK_GAPS, GRID_GAPS = (3, 5), (5, 10)
ORDER = (5, 4, 1, 0, 7, 6, 3, 2)

NT = (((1,), (1,)), ((), ()))
TN = (((0,), (0,)), ((), ()))
NN = (((1,), (0,)), ((), ()))


def dot(lhs, rhs, dims=NN):
    return lax.dot_general(lhs, rhs, dims, preferred_element_type=jnp.float32)


def layer_norm(values, gain):
    mean = jnp.mean(values, -1, keepdims=True)
    centred = values - mean
    spread = jnp.mean(centred * centred, -1, keepdims=True)
    return centred * lax.rsqrt(spread + 1e-05) * gain


def score_scale(hdim):
    return math.log2(math.e) / math.sqrt(hdim)


def head_mask(qlen, hdim):
    per = LANES // hdim
    row = lax.broadcasted_iota(jnp.int32, (per * qlen, LANES), 0) // qlen
    lane = lax.broadcasted_iota(jnp.int32, (per * qlen, LANES), 1) // hdim
    return jnp.where(row == lane, 1.0, 0.0).astype(jnp.bfloat16)


def pick_heads(mixed, qlen, hdim):
    return jnp.concatenate(
        [
            mixed[h * hdim : (h + 1) * hdim, h * qlen : (h + 1) * qlen]
            for h in range(LANES // hdim)
        ],
        0,
    )


def attend_windows(qkv, reg_keys, reg_values, windows, qlen, mask, hdim, gaps, beside={}):
    dim = reg_keys.shape[1]
    units = [(w, slice(lo, lo + LANES)) for w in windows for lo in range(0, dim, LANES)]
    tops, totals, done, held, weights = {}, {}, {}, {}, {}

    def scores(n):
        w, part = units[n]
        own = qkv[w * qlen : (w + 1) * qlen]
        keys = jnp.concatenate([own[:, dim : 2 * dim][:, part], reg_keys[:, part]], 0)
        stacked = jnp.concatenate([own[:, part]] * (LANES // hdim), 0) * mask
        result = dot(keys, stacked, NT)
        held[n] = result
        tops[n] = jnp.max(result, 0, keepdims=True)

    def exponentials(n):
        expo = jnp.exp2(held.pop(n) - tops[n])
        totals[n] = 1.0 / jnp.sum(expo, 0, keepdims=True)
        weights[n] = expo.astype(jnp.bfloat16)

    def weighted(n):
        w, part = units[n]
        own = qkv[w * qlen : (w + 1) * qlen]
        values = jnp.concatenate([own[:, 2 * dim :][:, part], reg_values[:, part]], 0)
        mixed = dot(values, weights.pop(n), TN) * totals[n]
        done[n] = pick_heads(mixed, qlen, hdim)

    to_expo, to_mixed = gaps
    for n in range(len(units) + to_mixed):
        if n < len(units):
            scores(n)
        if 0 <= n - to_expo < len(units):
            exponentials(n - to_expo)
        if 0 <= n - to_mixed:
            weighted(n - to_mixed)
        if n in beside:
            beside[n]()
    per = dim // LANES
    return [
        jnp.concatenate([done[i * per + g] for g in range(per)], 0) for i in range(len(windows))
    ]


def register_stages(query, keys, values, hdim, finish):
    dim = query.shape[1]
    held = {}

    def scores():
        mask = head_mask(REG, hdim)
        per = LANES // hdim
        parts = []
        for lo in range(0, dim, LANES):
            stacked = jnp.concatenate([query[:, lo : lo + LANES]] * per, 0) * mask
            parts.append(dot(keys[:, lo : lo + LANES], stacked, NT))
        held["scores"] = jnp.concatenate(parts, 1)

    def weights():
        top = jnp.max(held["scores"], 0, keepdims=True)
        expo = jnp.exp2(held.pop("scores") - top)
        held["weights"] = (expo * (1.0 / jnp.sum(expo, 0, keepdims=True))).astype(jnp.bfloat16)

    def mixed():
        result = dot(held.pop("weights"), values, TN)
        lane = lax.broadcasted_iota(jnp.int32, (REG, dim), 1) // hdim
        picked = jnp.zeros((REG, dim), jnp.float32)
        for h in range(HEADS):
            picked = jnp.where(lane == h, result[h * REG : (h + 1) * REG], picked)
        held["picked"] = picked.astype(jnp.bfloat16)

    return [scores, weights, mixed, lambda: finish(held["picked"])]


def block_kernel(
    x_hbm, reg_hbm, gain_hbm, gain_two_hbm, wqkv_hbm, wout_hbm,
    out_ref, reg_out_hbm,
    reg_out_ref, x_ref, reg_ref, gain_ref, gain_two_ref, wqkv_ref, wout_ref, sems,
):
    dim = x_ref.shape[2]
    parts = [slice(0, 2 * dim), slice(2 * dim, 3 * dim)]
    pairs = [
        (x_hbm, x_ref), (reg_hbm, reg_ref), (gain_hbm, gain_ref),
        *((wqkv_hbm.at[:, part], wqkv_ref.at[:, part]) for part in parts),
        (wout_hbm, wout_ref), (gain_two_hbm, gain_two_ref),
    ]
    copies = [pltpu.make_async_copy(src, dst, sems.at[i]) for i, (src, dst) in enumerate(pairs)]
    for copy in copies:
        copy.start()
    for copy in copies[:3]:
        copy.wait()
    rows, width, dim = x_ref.shape
    hdim = dim // HEADS
    count = width // WIN
    gain = gain_ref[...]
    values = x_ref[...].astype(jnp.float32)
    tokens = jnp.concatenate(
        [values[:, w * WIN : (w + 1) * WIN, :].reshape(rows * WIN, dim) for w in range(count)], 0
    )
    normed = layer_norm(tokens, gain).astype(jnp.bfloat16)
    reg_normed = layer_norm(reg_ref[...], gain).astype(jnp.bfloat16)
    everything = jnp.concatenate([normed, reg_normed], 0)
    copies[3].wait()
    early = dot(everything, wqkv_ref[:, parts[0]])
    early = jnp.concatenate([early[:, :dim] * score_scale(hdim), early[:, dim:]], 1)
    for copy in copies[4:]:
        copy.wait()
    late = dot(everything, wqkv_ref[:, parts[1]])
    both = jnp.concatenate([early.astype(jnp.bfloat16), late.astype(jnp.bfloat16)], 1)
    qkv, reg_qkv = both[: rows * width], both[rows * width :]

    leaving = pltpu.make_async_copy(reg_out_ref, reg_out_hbm, sems.at[7])

    def finish(reg_att):
        reg_out = reg_ref[...] + dot(reg_att, wout_ref[...])
        reg_out_ref[...] = reg_out
        leaving.start()
        travelling = layer_norm(reg_out, gain_two_ref[...]).astype(jnp.bfloat16)
        for r in range(rows):
            out_ref[r, width:, :] = travelling

    stages = register_stages(
        reg_qkv[:, :dim],
        jnp.concatenate([qkv[:, dim : 2 * dim], reg_qkv[:, dim : 2 * dim]], 0),
        jnp.concatenate([qkv[:, 2 * dim :], reg_qkv[:, 2 * dim :]], 0),
        hdim,
        finish,
    )
    qlen = rows * WIN
    mask = head_mask(qlen, hdim)
    reg_keys, reg_values = reg_qkv[:, dim : 2 * dim], reg_qkv[:, 2 * dim :]
    atts = attend_windows(
        qkv, reg_keys, reg_values, range(count), qlen, mask, hdim, BLOCK_GAPS, dict(zip(STAGE_AT, stages))
    )
    att = jnp.concatenate([each.T.astype(jnp.bfloat16) for each in atts], 0)
    result = tokens + dot(att, wout_ref[...])
    for w in range(count):
        piece = result[w * qlen : (w + 1) * qlen].reshape(rows, WIN, dim)
        out_ref[:, w * WIN : (w + 1) * WIN, :] = piece.astype(jnp.bfloat16)
    leaving.wait()


def grid_kernel(x_ref, gain_ref, wqkv_ref, wout_ref, out_ref, scratch):
    _, width, dim = out_ref.shape
    cls = width // WIN
    hdim = dim // HEADS
    qlen = WIN * WIN
    step = 4 if cls % 4 == 0 else 1
    gain = gain_ref[...]
    regs = jnp.concatenate([x_ref[a, width:, :] for a in range(WIN)], 0)
    reg_kv = dot(regs, wqkv_ref[:, dim:]).astype(jnp.bfloat16)
    mask = head_mask(qlen, hdim)
    lanes = [slice(g * LANES, (g + 1) * LANES) for g in range(dim // LANES)]
    for g, part in enumerate(lanes):
        for a in range(WIN):
            scratch[g, a * width : (a + 1) * width] = x_ref[a, :width, part].astype(jnp.float32)
    for first in range(0, cls, step):
        starts = [a * width + first + c for c in range(step) for a in range(WIN)]
        tokens = jnp.concatenate(
            [
                jnp.concatenate(
                    [scratch[g, pl.ds(start, WIN, stride=cls), :] for start in starts], 0
                )
                for g in range(len(lanes))
            ],
            1,
        )
        normed = layer_norm(tokens, gain).astype(jnp.bfloat16)
        qkv = jnp.concatenate(
            [
                (dot(normed, wqkv_ref[:, :dim]) * score_scale(hdim)).astype(jnp.bfloat16),
                dot(normed, wqkv_ref[:, dim:]).astype(jnp.bfloat16),
            ],
            1,
        )
        atts = attend_windows(
            qkv, reg_kv[:, :dim], reg_kv[:, dim:], range(step), qlen, mask, hdim, GRID_GAPS
        )
        att = jnp.concatenate([each.T.astype(jnp.bfloat16) for each in atts], 0)
        result = tokens + dot(att, wout_ref[...])
        for i, start in enumerate(starts):
            for g, part in enumerate(lanes):
                scratch[g, pl.ds(start, WIN, stride=cls), :] = result[i * WIN : (i + 1) * WIN, part]
    for g, part in enumerate(lanes):
        for a in range(WIN):
            out_ref[a, :, part] = scratch[g, a * width : (a + 1) * width].astype(jnp.bfloat16)


def call(kernel, outs, scratch=(), flops=0, **specs):
    return pl.pallas_call(
        kernel,
        out_shape=outs,
        scratch_shapes=list(scratch),
        compiler_params=pltpu.CompilerParams(vmem_limit_bytes=40 << 20),
        cost_estimate=pl.CostEstimate(flops=flops, bytes_accessed=4 << 20, transcendentals=0),
        **specs,
    )


def on_device(patches, registers, gain_one, gain_two, w_qkv_one, w_out_one, w_qkv_two, w_out_two):
    rows, width, dim = patches.shape
    nrow = lax.axis_size("row")
    per_band = nrow // WIN
    count = rows * width
    groups = [[a * per_band + p for a in ORDER] for p in range(per_band)]

    def exchange(values):
        return lax.all_to_all(
            values, "row", 0, 0, axis_index_groups=groups, tiled=True
        )

    bf16, f32 = jnp.bfloat16, jnp.float32
    shape = jax.ShapeDtypeStruct
    g_one, g_two = gain_one.reshape(1, dim), gain_two.reshape(1, dim)
    fetched = [
        pltpu.with_memory_space_constraint(value, pltpu.MemorySpace.HBM)
        for value in (patches, registers, g_one, g_two, w_qkv_one, w_out_one)
    ]
    outgoing, reg_out = call(
        block_kernel,
        (shape((rows, width + REG, dim), bf16), shape((REG, dim), f32)),
        [
            pltpu.VMEM((REG, dim), f32),
            pltpu.VMEM((rows, width, dim), bf16),
            pltpu.VMEM((REG, dim), f32),
            pltpu.VMEM((1, dim), f32),
            pltpu.VMEM((1, dim), f32),
            pltpu.VMEM((dim, 3 * dim), bf16),
            pltpu.VMEM((dim, dim), bf16),
            pltpu.SemaphoreType.DMA((8,)),
        ],
        flops=2 * count * dim * 4 * dim,
        in_specs=[pl.BlockSpec(memory_space=pltpu.MemorySpace.HBM)] * 6,
        out_specs=(
            pl.BlockSpec(memory_space=pltpu.MemorySpace.VMEM),
            pl.BlockSpec(memory_space=pltpu.MemorySpace.HBM),
        ),
    )(*fetched)
    finished = call(
        grid_kernel,
        shape((rows, width, dim), bf16),
        [
            pltpu.VMEM((dim // LANES, count, LANES), f32),
        ],
        flops=2 * count * dim * 6 * dim,
    )(exchange(outgoing), g_two, w_qkv_two, w_out_two)
    patches_out = exchange(finished)
    return (patches_out, reg_out)


def solution(mesh):
    in_specs = (
        P(("grp", "row"), None, None),
        P(("grp", "row"), None),
        P(),
        P(),
        P(),
        P(),
        P(),
        P(),
    )
    out_specs = (P(("grp", "row"), None, None), P(("grp", "row"), None))
    return jax.shard_map(
        on_device, mesh=mesh, in_specs=in_specs, out_specs=out_specs, check_vma=False
    )
```
